32 devices in a mesh: round: 2 (over x), seq: 16 (over z, y, core).
Axes of the slice: x: 2, y: 2, z: 4, core: 2. Of those that a mesh axis runs over, the one named last changes fastest.
Arguments:
- qk: bfloat16 [8192, 1024], P('seq'), may hold values from -96 to 96
- values: bfloat16 [8192, 1024], P('seq'), may hold values from -6 to 6
- dest_dev: int32 [2, 8192], P('round', 'seq'), may hold values from 0 to 15, as said below
- dest_slot: int32 [2, 8192], P('round', 'seq'), may hold values from 0 to 511, as said below
Outputs:
- merged: bfloat16 [8192, 1024], P('seq', 'round')
The draws below stay inside these ranges and needn't reach their ends.
Inputs may be any that keep to these rules, and one draw needn't show every extreme that they name: dest_dev and dest_slot together send each round's 8192 tokens to 8192 distinct positions. In each round, from the rows of one index of seq at most 48 go to any one index of seq, and exactly 48 for some pair; every index receives exactly 512 rows. `dest_slot`: the row within the destination's block, see dest_dev.
All inputs are finite; a program needn't handle non-finite values.
Results may differ from the reference program's by a relative error of at most 0.03.
Values may be sent and summed in bfloat16 or wider, within the bound.
A program may use at most 64 MiB of HBM per device.

```python
import jax
import jax.numpy as jnp
from jax import lax

D = 1024
HEADS = 8
HEAD_DIM = 128
STRETCH = 512
TOK_DEV = 512
ROUNDS = 2
TOKENS = 8192
HALF = 16
N_SEQ = 16


def route_round(key):
    shards = N_SEQ
    keys = jax.random.split(key, 6)
    lifts = jax.random.randint(keys[0], (shards // 2,), 0, HALF + 1)
    lifts = lifts.at[0].set(HALF)
    offsets = jnp.concatenate([lifts, -lifts])[jax.random.permutation(keys[1], shards)]
    sigma = jax.random.permutation(keys[2], shards)
    shuffle = jax.random.permutation(keys[3], shards)
    counts = 2 * HALF + offsets[(shuffle[None, :] - sigma[:, None]) % shards]
    ends = jnp.cumsum(counts, axis=1)
    starts = ends - counts
    spots = jnp.arange(TOK_DEV, dtype=jnp.int32)
    target = jnp.sum((spots[None, :, None] >= ends[:, None, :]).astype(jnp.int32), axis=2)
    ranks = spots[None, :] - jnp.take_along_axis(starts, target, axis=1)
    incoming = jnp.cumsum(counts, axis=0) - counts
    arrival = jnp.take_along_axis(incoming, target, axis=1) + ranks
    slot_orders = jax.vmap(lambda k: jax.random.permutation(k, TOK_DEV))(jax.random.split(keys[4], shards))
    slots = slot_orders[target, arrival]
    row_orders = jax.vmap(lambda k: jax.random.permutation(k, TOK_DEV))(jax.random.split(keys[5], shards))
    sources = jnp.arange(shards, dtype=jnp.int32)[:, None]
    dests = jnp.zeros((shards, TOK_DEV), jnp.int32).at[sources, row_orders].set(target.astype(jnp.int32))
    places = jnp.zeros((shards, TOK_DEV), jnp.int32).at[sources, row_orders].set(slots.astype(jnp.int32))
    return (dests.reshape(-1), places.reshape(-1))


def routing(key):
    base = jax.random.fold_in(key, 7001)
    return jax.vmap(route_round)(jax.random.split(base, ROUNDS))


def draw_dest_dev(key, part):
    return routing(key)[0]


def draw_dest_slot(key, part):
    return routing(key)[1]


def draw_qk(key, part):
    noise_key = jax.random.fold_in(key, 11)
    field = jax.random.truncated_normal(noise_key, -6.0, 6.0, (TOKENS, D))
    return field.astype(jnp.bfloat16)


def block_scale(key, shape, pieces, smallest, high):
    def one(axis_at, shards_of):
        steps = jax.random.uniform(jax.random.fold_in(jax.random.fold_in(key, 6), axis_at), (shards_of,), jnp.float32, smallest / len(pieces), high / len(pieces))
        return jnp.repeat(jnp.exp(steps), shape[axis_at] // shards_of).reshape((-1,) + (1,) * (len(shape) - axis_at - 1))

    gain = one(*pieces[0])
    for cut in pieces[1:]:
        gain = gain * one(*cut)
    return gain


def normal_values(stream_key, shape, spread, bound, cuts=(), held_as=jnp.bfloat16):
    array = spread * jax.random.normal(stream_key, shape, jnp.float32)
    if cuts:
        array = array * block_scale(stream_key, shape, cuts, -0.22, 0.18)
    return jnp.clip(array, -bound, bound).astype(held_as)


def setup_inputs(seed: int = 0) -> dict:
    arg_keys = jax.random.split(jax.random.key(seed), 5)
    qk = draw_qk(jax.random.fold_in(arg_keys[4], 71), 0)
    values = normal_values(arg_keys[1], (TOKENS, D), 1.0, 6.0, ((0, 16),))
    dest_dev = draw_dest_dev(jax.random.fold_in(arg_keys[4], 71), 0)
    dest_slot = draw_dest_slot(jax.random.fold_in(arg_keys[4], 71), 0)
    return dict(qk=qk, values=values, dest_dev=dest_dev, dest_slot=dest_slot)


eps_norm = 1e-06
self_score = -100000.0

def unit_keys(rows):
    count = rows.shape[0]
    heads = rows.shape[1] // HEAD_DIM
    field = rows.astype(jnp.float32).reshape(count, heads, HEAD_DIM)
    field = field * lax.rsqrt(lax.optimization_barrier(jnp.sum(field * field, axis=-1, keepdims=True)) + eps_norm)
    return field.reshape(count, heads * HEAD_DIM).astype(jnp.bfloat16)

def window_attend(queries, keys, vals):
    rows = queries.shape[0]
    heads = queries.shape[1] // HEAD_DIM
    qcast = queries.astype(jnp.float32).reshape(rows, heads, HEAD_DIM)
    kcast = keys.astype(jnp.float32).reshape(2 * rows, heads, HEAD_DIM)
    vcast = vals.astype(jnp.float32).reshape(2 * rows, heads, HEAD_DIM)
    scores = jnp.einsum('qhd,khd->hqk', qcast, kcast)
    itself = jnp.arange(2 * rows, dtype=jnp.int32)[None, :] == jnp.arange(rows, dtype=jnp.int32)[:, None] + rows
    scores = jnp.where(itself[None], jnp.float32(self_score), scores)
    highest = lax.optimization_barrier(jnp.max(scores, axis=-1))
    lse = highest + jnp.log(lax.optimization_barrier(jnp.sum(jnp.exp(scores - highest[..., None]), axis=-1)))
    probs = jnp.exp(scores - lse[..., None]).astype(jnp.bfloat16)
    attended = jnp.einsum('hqk,khd->qhd', probs.astype(jnp.float32), vcast)
    return (attended.reshape(rows, heads * HEAD_DIM).astype(jnp.bfloat16), jnp.transpose(lse))

def reference(qk, values, dest_dev, dest_slot):
    count = TOKENS // STRETCH
    outs = []
    lses = []
    for index in range(ROUNDS):
        place = (dest_dev[index] * TOK_DEV + dest_slot[index]).astype(jnp.int32)
        inverse = jnp.zeros((TOKENS,), jnp.int32).at[place].set(jnp.arange(TOKENS, dtype=jnp.int32))
        sorted_qk = qk[inverse]
        sorted_values = values[inverse]
        keys = unit_keys(sorted_qk)
        ext_keys = jnp.concatenate([keys[-STRETCH:], keys], axis=0)
        ext_values = jnp.concatenate([sorted_values[-STRETCH:], sorted_values], axis=0)

        def one_stretch(position):
            start = (position * STRETCH).astype(jnp.int32)
            queries = lax.dynamic_slice_in_dim(sorted_qk, start, STRETCH, 0)
            window_keys = lax.dynamic_slice_in_dim(ext_keys, start, 2 * STRETCH, 0)
            window_values = lax.dynamic_slice_in_dim(ext_values, start, 2 * STRETCH, 0)
            return window_attend(queries, window_keys, window_values)
        attended, lse = lax.map(one_stretch, jnp.arange(count, dtype=jnp.int32))
        attended = attended.reshape(TOKENS, D)
        lse = lse.reshape(TOKENS, HEADS)
        outs.append(attended[place])
        lses.append(lse[place])
    stacked = jnp.stack(lses)
    highest = lax.optimization_barrier(jnp.max(stacked, axis=0))
    total = highest + jnp.log(lax.optimization_barrier(jnp.sum(jnp.exp(stacked - highest[None]), axis=0)))
    merged = jnp.zeros((TOKENS, D), jnp.float32)
    for index in range(ROUNDS):
        weight = jnp.repeat(jnp.exp(lses[index] - total), HEAD_DIM, axis=1)
        merged = merged + weight * outs[index].astype(jnp.float32)
    return merged.astype(jnp.bfloat16)
```

```python
import jax
import jax.numpy as jnp
from jax import lax
from jax.experimental import pallas as pl
from jax.experimental.pallas import tpu as pltpu
from jax.sharding import PartitionSpec as P

HEAD_DIM = 128
STRETCH = 512


eps_norm = 1e-06
self_score = -100000.0


def passed_along(value, axis, steps):
    count = lax.axis_size(axis)
    pairs = [(source, (source + steps) % count) for source in range(count)]
    return lax.ppermute(value, axis, pairs)


def as_sent(array):
    return jax.tree.map(lambda a: a.astype(jnp.bfloat16) if a.dtype == jnp.float32 else a, array)


def unit_keys(rows):
    count = rows.shape[0]
    heads = rows.shape[1] // HEAD_DIM
    field = rows.astype(jnp.float32).reshape(count, heads, HEAD_DIM)
    field = field * lax.rsqrt(jnp.sum(field * field, axis=-1, keepdims=True) + eps_norm)
    return field.reshape(count, heads * HEAD_DIM).astype(jnp.bfloat16)


def spread_heads(weights):
    return jnp.repeat(weights, HEAD_DIM, axis=1)


def pack_round(qk, values, dest, slot, shards, cap):
    rows = qk.shape[0]
    hits = (dest[:, None] == jnp.arange(shards, dtype=jnp.int32)[None, :]).astype(jnp.int32)
    ranks = jnp.sum(hits * jnp.cumsum(hits, axis=0), axis=1) - 1
    position = dest * cap + ranks
    total = shards * cap
    send_qk = jnp.zeros((total, qk.shape[1]), qk.dtype).at[position].set(qk)
    send_values = jnp.zeros((total, values.shape[1]), values.dtype).at[position].set(values)
    send_slot = jnp.full((total,), rows, jnp.int32).at[position].set(slot)
    send_source = (
        jnp.full((total,), rows, jnp.int32).at[position].set(jnp.arange(rows, dtype=jnp.int32))
    )
    return (send_qk, send_values, send_slot, send_source)


def group_attend(queries, keys, vals):
    rows = queries.shape[0]
    heads = queries.shape[1] // HEAD_DIM
    qpart = queries.reshape(rows, heads, HEAD_DIM)
    kpart = keys.reshape(2 * rows, heads, HEAD_DIM)
    vpart = vals.reshape(2 * rows, heads, HEAD_DIM)
    scores = jnp.einsum("qhd,khd->hqk", qpart, kpart, preferred_element_type=jnp.float32)
    itself = (
        jnp.arange(2 * rows, dtype=jnp.int32)[None, :]
        == jnp.arange(rows, dtype=jnp.int32)[:, None] + rows
    )
    scores = jnp.where(itself[None], jnp.float32(self_score), scores)
    highest = jnp.max(scores, axis=-1)
    lse = highest + jnp.log(jnp.sum(jnp.exp(scores - highest[..., None]), axis=-1))
    probs = jnp.exp(scores - lse[..., None]).astype(jnp.bfloat16)
    attended = jnp.einsum("hqk,khd->qhd", probs, vpart, preferred_element_type=jnp.float32)
    return (attended.reshape(rows, heads * HEAD_DIM).astype(jnp.bfloat16), jnp.transpose(lse))


def attend_sorted(sorted_qk, sorted_values):
    rows = sorted_qk.shape[0]
    width = sorted_qk.shape[1]
    keys = unit_keys(sorted_qk)
    before_keys, before_values = passed_along((keys, sorted_values), "seq", 1)
    ext_keys = jnp.concatenate([before_keys, keys], axis=0)
    ext_values = jnp.concatenate([before_values, sorted_values], axis=0)
    group_width = width // 2

    def one_stretch(position):
        pieces = []
        totals = []
        for group in range(2):
            low = group * group_width
            high = low + group_width
            piece, total = group_attend(
                sorted_qk[:, low:high], ext_keys[:, low:high], ext_values[:, low:high]
            )
            pieces.append(piece)
            totals.append(total)
        return (jnp.concatenate(pieces, axis=1), jnp.concatenate(totals, axis=1))

    attended, lse = lax.map(one_stretch, jnp.arange(rows // STRETCH, dtype=jnp.int32))
    return (attended.reshape(rows, width), lse.reshape(rows, lse.shape[-1]))


def on_device(qk, values, dest_dev, dest_slot):
    shards = lax.axis_size("seq")
    rows = qk.shape[0]
    width = qk.shape[1]
    heads = width // HEAD_DIM
    cap = 3 * (rows // (2 * shards))
    send_qk, send_values, send_slot, send_source = pack_round(
        qk, values, dest_dev[0], dest_slot[0], shards, cap
    )
    got_qk, got_values, got_slot, got_source = (
        lax.all_to_all(send_qk, "seq", split_axis=0, concat_axis=0, tiled=True),
        lax.all_to_all(send_values, "seq", split_axis=0, concat_axis=0, tiled=True),
        lax.all_to_all(send_slot, "seq", split_axis=0, concat_axis=0, tiled=True),
        lax.all_to_all(send_source, "seq", split_axis=0, concat_axis=0, tiled=True),
    )
    sorted_qk = jnp.zeros((rows, width), jnp.bfloat16).at[got_slot].set(got_qk, mode="drop")
    sorted_values = jnp.zeros((rows, width), jnp.bfloat16).at[got_slot].set(got_values, mode="drop")
    attended, lse = attend_sorted(sorted_qk, sorted_values)
    lse = lse.reshape(rows, heads)
    picked = jnp.clip(got_slot, 0, rows - 1)
    reply_out = attended[picked]
    reply_lse = lse[picked]
    back_out, back_lse, back_ids = (
        lax.all_to_all(as_sent(reply_out), "seq", split_axis=0, concat_axis=0, tiled=True).astype(
            reply_out.dtype
        ),
        lax.all_to_all(as_sent(reply_lse), "seq", split_axis=0, concat_axis=0, tiled=True).astype(
            reply_lse.dtype
        ),
        lax.all_to_all(got_source, "seq", split_axis=0, concat_axis=0, tiled=True),
    )
    round_out = jnp.zeros((rows, width), jnp.bfloat16).at[back_ids].set(back_out, mode="drop")
    round_lse = jnp.zeros((rows, heads), jnp.float32).at[back_ids].set(back_lse, mode="drop")
    local_top = round_lse
    local_top = lax.pmax(local_top, "round")
    denom = jnp.exp(round_lse - local_top)
    numer = spread_heads(denom) * round_out.astype(jnp.float32)
    numer_half, denom_half = (
        lax.psum_scatter(
            numer.astype(jnp.bfloat16), "round", scatter_dimension=1, tiled=True
        ).astype(jnp.float32),
        lax.psum_scatter(
            denom.astype(jnp.bfloat16), "round", scatter_dimension=1, tiled=True
        ).astype(jnp.float32),
    )
    merged = numer_half / spread_heads(denom_half)
    return merged.astype(jnp.bfloat16)


NO_ROW = -1e30
CHUNK = 16


def by_head(array, side, heads):
    wide = heads * HEAD_DIM
    part = lax.dynamic_slice_in_dim(array, side * wide, wide, 1)
    return jnp.transpose(part.reshape(array.shape[0], heads, HEAD_DIM), (1, 0, 2))


def local_kernel(
    put_ref, take_ref, tokens_ref, out_ref, lse_ref, wide_q, wide_v, sorted_q, sorted_v, att, logs
):
    blocks, _, rows, _ = tokens_ref.shape
    bound = sorted_q.shape[0] - 8

    @pl.loop(0, blocks)
    def _(block):
        wide_q[...] = tokens_ref[block, 0].astype(jnp.float32)
        wide_v[...] = tokens_ref[block, 1].astype(jnp.float32)

        @pl.loop(0, rows, step=CHUNK)
        def _(start):
            for row in range(CHUNK):
                to = put_ref[block * rows + start + row]
                sorted_q[pl.ds(to, 1), :] = wide_q[pl.ds(start + row, 1), :]
                sorted_v[pl.ds(to, 1), :] = wide_v[pl.ds(start + row, 1), :]

    att[pl.ds(bound, 8), :] = jnp.zeros((8, HEAD_DIM), jnp.float32)
    logs[pl.ds(bound, 8), :] = jnp.full((8, HEAD_DIM), NO_ROW, jnp.float32)

    @pl.loop(0, bound // STRETCH - 1)
    def _(stretch):
        low = pl.multiple_of(stretch * STRETCH, STRETCH)
        own = pl.multiple_of(low + STRETCH, STRETCH)
        queries = sorted_q[pl.ds(own, STRETCH), :].astype(jnp.bfloat16)
        field = sorted_q[pl.ds(low, 2 * STRETCH), :]
        scale = lax.rsqrt(jnp.sum(field * field, axis=-1, keepdims=True) + eps_norm)
        keys = (field * scale).astype(jnp.bfloat16)
        vals = sorted_v[pl.ds(low, 2 * STRETCH), :].astype(jnp.bfloat16)
        scores = lax.dot_general(
            queries, keys, (((1,), (1,)), ((), ())), preferred_element_type=jnp.float32
        )
        row_at = lax.broadcasted_iota(jnp.int32, scores.shape, 0) + STRETCH
        col_at = lax.broadcasted_iota(jnp.int32, scores.shape, 1)
        scores = jnp.where(row_at == col_at, jnp.float32(self_score), scores)
        highest = jnp.max(scores, axis=-1, keepdims=True)
        probs = jnp.exp(scores - highest)
        weight = jnp.sum(probs, axis=-1, keepdims=True)
        attended = jnp.dot(probs.astype(jnp.bfloat16), vals, preferred_element_type=jnp.float32)
        att[pl.ds(own, STRETCH), :] = attended / weight
        logs[pl.ds(own, STRETCH), :] = jnp.broadcast_to(
            highest + jnp.log(weight), (STRETCH, HEAD_DIM)
        )

    @pl.loop(0, blocks)
    def _(block):
        @pl.loop(0, rows, step=CHUNK)
        def _(start):
            for row in range(CHUNK):
                at = take_ref[block * rows + start + row]
                wide_q[pl.ds(start + row, 1), :] = att[pl.ds(at, 1), :]
                wide_v[pl.ds(start + row, 1), :] = logs[pl.ds(at, 1), :]

        out_ref[block] = wide_q[...].astype(jnp.bfloat16)
        lse_ref[block] = jnp.transpose(wide_v[...])[0:1, :]


def local_attend(put, take, tokens, section):
    blocks, _, rows, wide = tokens.shape
    bound = section + STRETCH + 8
    return pl.pallas_call(
        local_kernel,
        out_shape=(
            jax.ShapeDtypeStruct((blocks, rows, wide), jnp.bfloat16),
            jax.ShapeDtypeStruct((blocks, 1, rows), jnp.float32),
        ),
        in_specs=[
            pl.BlockSpec(memory_space=pltpu.SMEM),
            pl.BlockSpec(memory_space=pltpu.SMEM),
            pl.BlockSpec(memory_space=pltpu.VMEM),
        ],
        out_specs=(
            pl.BlockSpec(memory_space=pltpu.VMEM),
            pl.BlockSpec(memory_space=pltpu.VMEM),
        ),
        scratch_shapes=[
            pltpu.VMEM((rows, wide), jnp.float32),
            pltpu.VMEM((rows, wide), jnp.float32),
            pltpu.VMEM((bound, wide), jnp.float32),
            pltpu.VMEM((bound, wide), jnp.float32),
            pltpu.VMEM((bound, wide), jnp.float32),
            pltpu.VMEM((bound, wide), jnp.float32),
        ],
        compiler_params=pltpu.CompilerParams(vmem_limit_bytes=48 * 1024 * 1024),
        name="local_attend",
    )(put, take, tokens)


def head_groups(shards, heads):
    group = shards // heads
    along = [[lane + group * step for step in range(heads)] for lane in range(group)]
    within = [[group * step + lane for lane in range(group)] for step in range(heads)]
    return group, along, within


def slots_of(place, section, base, total):
    bound = section + STRETCH
    put = jnp.minimum(lax.rem(place - base + STRETCH + total, total), bound)
    take = jnp.where(put < STRETCH, bound, put)
    return put, take


def by_heads_on_device(qk, values, dest_dev, dest_slot):
    shards = lax.axis_size("seq")
    sides = lax.axis_size("round")
    rows, width = qk.shape
    heads = width // HEAD_DIM // sides
    total = rows * shards
    group, along, within = head_groups(shards, heads)
    parts = group // sides
    section = total // parts
    side = lax.axis_index("round")
    lane = lax.rem(lax.axis_index("seq"), group)
    place = dest_dev[0] * rows + dest_slot[0]
    places = lax.all_gather(place, ("round", "seq")).reshape(sides, shards, rows)
    mine = lax.dynamic_index_in_dim(places, lane // parts, 0, keepdims=False)
    mine = jnp.transpose(mine.reshape(heads, group, rows), (1, 0, 2)).reshape(-1)
    put, take = slots_of(mine, section, lax.rem(lane, parts) * section, total)
    packed = jnp.stack([by_head(qk, side, heads), by_head(values, side, heads)], axis=1)
    packed = lax.all_to_all(
        packed, "seq", split_axis=0, concat_axis=0, tiled=True, axis_index_groups=along
    )
    tokens = lax.all_gather(packed, "seq", axis_index_groups=within)
    tokens = tokens.reshape(shards, 2, rows, HEAD_DIM)
    out, lse = local_attend(put, take, tokens, section)
    out = lax.all_to_all(
        out, "seq", split_axis=0, concat_axis=0, tiled=True, axis_index_groups=within
    ).reshape(group, heads, rows, HEAD_DIM)
    lse = lax.all_to_all(
        lse, "seq", split_axis=0, concat_axis=0, tiled=True, axis_index_groups=within
    ).reshape(group, heads, rows)
    weight = jnp.exp(lse - jnp.max(lse, axis=0, keepdims=True))
    weight = weight / jnp.sum(weight, axis=0, keepdims=True)
    merged = jnp.sum(weight[..., None] * out.astype(jnp.float32), axis=0).astype(jnp.bfloat16)
    merged = lax.all_to_all(
        merged, "seq", split_axis=0, concat_axis=0, tiled=True, axis_index_groups=along
    )
    return jnp.transpose(merged, (1, 0, 2)).reshape(rows, heads * HEAD_DIM)


def whole_head_fits(qk, shards, sides):
    rows, width = qk.shape
    heads = width // HEAD_DIM // sides
    bytes_held = rows * HEAD_DIM * shards * 2 * 2
    if shards % heads or (shards // heads) % sides:
        return False
    parts = shards // heads // sides
    if (rows * shards) % (parts * STRETCH) or parts < 2:
        return False
    return bytes_held <= 8 * 1024 * 1024


def either_plan(qk, values, dest_dev, dest_slot):
    if whole_head_fits(qk, lax.axis_size("seq"), lax.axis_size("round")):
        return by_heads_on_device(qk, values, dest_dev, dest_slot)
    return on_device(qk, values, dest_dev, dest_slot)


def solution(mesh):
    return jax.shard_map(
        either_plan,
        mesh=mesh,
        in_specs=(P("seq", None), P("seq", None), P("round", "seq"), P("round", "seq")),
        out_specs=P("seq", "round"),
        check_vma=False,
    )
```

```python
import functools

import jax
import jax.numpy as jnp
from jax import lax
from jax.experimental import pallas as pl
from jax.experimental.pallas import tpu as pltpu
from jax.sharding import PartitionSpec as P

HEAD_DIM = 128
STRETCH = 512


eps_norm = 1e-06
self_score = -100000.0


def passed_along(value, axis, steps):
    count = lax.axis_size(axis)
    pairs = [(source, (source + steps) % count) for source in range(count)]
    return lax.ppermute(value, axis, pairs)


def as_sent(array):
    return jax.tree.map(lambda a: a.astype(jnp.bfloat16) if a.dtype == jnp.float32 else a, array)


def unit_keys(rows):
    count = rows.shape[0]
    heads = rows.shape[1] // HEAD_DIM
    field = rows.astype(jnp.float32).reshape(count, heads, HEAD_DIM)
    field = field * lax.rsqrt(jnp.sum(field * field, axis=-1, keepdims=True) + eps_norm)
    return field.reshape(count, heads * HEAD_DIM).astype(jnp.bfloat16)


def spread_heads(weights):
    return jnp.repeat(weights, HEAD_DIM, axis=1)


def pack_round(qk, values, dest, slot, shards, cap):
    rows = qk.shape[0]
    hits = (dest[:, None] == jnp.arange(shards, dtype=jnp.int32)[None, :]).astype(jnp.int32)
    ranks = jnp.sum(hits * jnp.cumsum(hits, axis=0), axis=1) - 1
    position = dest * cap + ranks
    total = shards * cap
    send_qk = jnp.zeros((total, qk.shape[1]), qk.dtype).at[position].set(qk)
    send_values = jnp.zeros((total, values.shape[1]), values.dtype).at[position].set(values)
    send_slot = jnp.full((total,), rows, jnp.int32).at[position].set(slot)
    send_source = (
        jnp.full((total,), rows, jnp.int32).at[position].set(jnp.arange(rows, dtype=jnp.int32))
    )
    return (send_qk, send_values, send_slot, send_source)


def group_attend(queries, keys, vals):
    rows = queries.shape[0]
    heads = queries.shape[1] // HEAD_DIM
    qpart = queries.reshape(rows, heads, HEAD_DIM)
    kpart = keys.reshape(2 * rows, heads, HEAD_DIM)
    vpart = vals.reshape(2 * rows, heads, HEAD_DIM)
    scores = jnp.einsum("qhd,khd->hqk", qpart, kpart, preferred_element_type=jnp.float32)
    itself = (
        jnp.arange(2 * rows, dtype=jnp.int32)[None, :]
        == jnp.arange(rows, dtype=jnp.int32)[:, None] + rows
    )
    scores = jnp.where(itself[None], jnp.float32(self_score), scores)
    highest = jnp.max(scores, axis=-1)
    lse = highest + jnp.log(jnp.sum(jnp.exp(scores - highest[..., None]), axis=-1))
    probs = jnp.exp(scores - lse[..., None]).astype(jnp.bfloat16)
    attended = jnp.einsum("hqk,khd->qhd", probs, vpart, preferred_element_type=jnp.float32)
    return (attended.reshape(rows, heads * HEAD_DIM).astype(jnp.bfloat16), jnp.transpose(lse))


def attend_sorted(sorted_qk, sorted_values):
    rows = sorted_qk.shape[0]
    width = sorted_qk.shape[1]
    keys = unit_keys(sorted_qk)
    before_keys, before_values = passed_along((keys, sorted_values), "seq", 1)
    ext_keys = jnp.concatenate([before_keys, keys], axis=0)
    ext_values = jnp.concatenate([before_values, sorted_values], axis=0)
    group_width = width // 2

    def one_stretch(position):
        pieces = []
        totals = []
        for group in range(2):
            low = group * group_width
            high = low + group_width
            piece, total = group_attend(
                sorted_qk[:, low:high], ext_keys[:, low:high], ext_values[:, low:high]
            )
            pieces.append(piece)
            totals.append(total)
        return (jnp.concatenate(pieces, axis=1), jnp.concatenate(totals, axis=1))

    attended, lse = lax.map(one_stretch, jnp.arange(rows // STRETCH, dtype=jnp.int32))
    return (attended.reshape(rows, width), lse.reshape(rows, lse.shape[-1]))


def on_device(qk, values, dest_dev, dest_slot):
    shards = lax.axis_size("seq")
    rows = qk.shape[0]
    width = qk.shape[1]
    heads = width // HEAD_DIM
    cap = 3 * (rows // (2 * shards))
    send_qk, send_values, send_slot, send_source = pack_round(
        qk, values, dest_dev[0], dest_slot[0], shards, cap
    )
    got_qk, got_values, got_slot, got_source = (
        lax.all_to_all(send_qk, "seq", split_axis=0, concat_axis=0, tiled=True),
        lax.all_to_all(send_values, "seq", split_axis=0, concat_axis=0, tiled=True),
        lax.all_to_all(send_slot, "seq", split_axis=0, concat_axis=0, tiled=True),
        lax.all_to_all(send_source, "seq", split_axis=0, concat_axis=0, tiled=True),
    )
    sorted_qk = jnp.zeros((rows, width), jnp.bfloat16).at[got_slot].set(got_qk, mode="drop")
    sorted_values = jnp.zeros((rows, width), jnp.bfloat16).at[got_slot].set(got_values, mode="drop")
    attended, lse = attend_sorted(sorted_qk, sorted_values)
    lse = lse.reshape(rows, heads)
    picked = jnp.clip(got_slot, 0, rows - 1)
    reply_out = attended[picked]
    reply_lse = lse[picked]
    back_out, back_lse, back_ids = (
        lax.all_to_all(as_sent(reply_out), "seq", split_axis=0, concat_axis=0, tiled=True).astype(
            reply_out.dtype
        ),
        lax.all_to_all(as_sent(reply_lse), "seq", split_axis=0, concat_axis=0, tiled=True).astype(
            reply_lse.dtype
        ),
        lax.all_to_all(got_source, "seq", split_axis=0, concat_axis=0, tiled=True),
    )
    round_out = jnp.zeros((rows, width), jnp.bfloat16).at[back_ids].set(back_out, mode="drop")
    round_lse = jnp.zeros((rows, heads), jnp.float32).at[back_ids].set(back_lse, mode="drop")
    local_top = round_lse
    local_top = lax.pmax(local_top, "round")
    denom = jnp.exp(round_lse - local_top)
    numer = spread_heads(denom) * round_out.astype(jnp.float32)
    numer_half, denom_half = (
        lax.psum_scatter(
            numer.astype(jnp.bfloat16), "round", scatter_dimension=1, tiled=True
        ).astype(jnp.float32),
        lax.psum_scatter(
            denom.astype(jnp.bfloat16), "round", scatter_dimension=1, tiled=True
        ).astype(jnp.float32),
    )
    merged = numer_half / spread_heads(denom_half)
    return merged.astype(jnp.bfloat16)


NO_ROW = -1e30
CHUNK = 16


def local_kernel(
    put_ref, take_ref, tokens_ref, out_ref, lse_ref, wide_q, wide_v, sorted_q, sorted_v, att, logs
):
    blocks, _, rows, _ = tokens_ref.shape
    bound = sorted_q.shape[0] - 8

    @pl.loop(0, blocks)
    def _(block):
        wide_q[...] = tokens_ref[block, 0].astype(jnp.float32)
        wide_v[...] = tokens_ref[block, 1].astype(jnp.float32)

        @pl.loop(0, rows, step=CHUNK)
        def _(start):
            for row in range(CHUNK):
                to = put_ref[block * rows + start + row]
                sorted_q[pl.ds(to, 1), :] = wide_q[pl.ds(start + row, 1), :]
                sorted_v[pl.ds(to, 1), :] = wide_v[pl.ds(start + row, 1), :]

    att[pl.ds(bound, 8), :] = jnp.zeros((8, HEAD_DIM), jnp.float32)
    logs[pl.ds(bound, 8), :] = jnp.full((8, HEAD_DIM), NO_ROW, jnp.float32)

    @pl.loop(0, bound // STRETCH - 1)
    def _(stretch):
        low = pl.multiple_of(stretch * STRETCH, STRETCH)
        own = pl.multiple_of(low + STRETCH, STRETCH)
        queries = sorted_q[pl.ds(own, STRETCH), :].astype(jnp.bfloat16)
        field = sorted_q[pl.ds(low, 2 * STRETCH), :]
        scale = lax.rsqrt(jnp.sum(field * field, axis=-1, keepdims=True) + eps_norm)
        keys = (field * scale).astype(jnp.bfloat16)
        vals = sorted_v[pl.ds(low, 2 * STRETCH), :].astype(jnp.bfloat16)
        scores = lax.dot_general(
            queries, keys, (((1,), (1,)), ((), ())), preferred_element_type=jnp.float32
        )
        row_at = lax.broadcasted_iota(jnp.int32, scores.shape, 0) + STRETCH
        col_at = lax.broadcasted_iota(jnp.int32, scores.shape, 1)
        scores = jnp.where(row_at == col_at, jnp.float32(self_score), scores)
        highest = jnp.max(scores, axis=-1, keepdims=True)
        probs = jnp.exp(scores - highest)
        weight = jnp.sum(probs, axis=-1, keepdims=True)
        attended = jnp.dot(probs.astype(jnp.bfloat16), vals, preferred_element_type=jnp.float32)
        att[pl.ds(own, STRETCH), :] = attended / weight
        logs[pl.ds(own, STRETCH), :] = jnp.broadcast_to(
            highest + jnp.log(weight), (STRETCH, HEAD_DIM)
        )

    @pl.loop(0, blocks)
    def _(block):
        @pl.loop(0, rows, step=CHUNK)
        def _(start):
            for row in range(CHUNK):
                at = take_ref[block * rows + start + row]
                wide_q[pl.ds(start + row, 1), :] = att[pl.ds(at, 1), :]
                wide_v[pl.ds(start + row, 1), :] = logs[pl.ds(at, 1), :]

        out_ref[block] = wide_q[...].astype(jnp.bfloat16)
        lse_ref[block] = jnp.transpose(wide_v[...])[0:1, :]


def local_attend(put, take, tokens, section):
    blocks, _, rows, wide = tokens.shape
    bound = section + STRETCH + 8
    return pl.pallas_call(
        local_kernel,
        out_shape=(
            jax.ShapeDtypeStruct((blocks, rows, wide), jnp.bfloat16),
            jax.ShapeDtypeStruct((blocks, 1, rows), jnp.float32),
        ),
        in_specs=[
            pl.BlockSpec(memory_space=pltpu.SMEM),
            pl.BlockSpec(memory_space=pltpu.SMEM),
            pl.BlockSpec(memory_space=pltpu.VMEM),
        ],
        out_specs=(
            pl.BlockSpec(memory_space=pltpu.VMEM),
            pl.BlockSpec(memory_space=pltpu.VMEM),
        ),
        scratch_shapes=[
            pltpu.VMEM((rows, wide), jnp.float32),
            pltpu.VMEM((rows, wide), jnp.float32),
            pltpu.VMEM((bound, wide), jnp.float32),
            pltpu.VMEM((bound, wide), jnp.float32),
            pltpu.VMEM((bound, wide), jnp.float32),
            pltpu.VMEM((bound, wide), jnp.float32),
        ],
        compiler_params=pltpu.CompilerParams(vmem_limit_bytes=48 * 1024 * 1024),
        name="local_attend",
    )(put, take, tokens)


MESH = pl.DeviceIdType.MESH


def near_first(count):
    return sorted(range(1, count), key=lambda step: min(step, count - step))


def greet_all(sides, shards, side, seat):
    barrier = pltpu.get_barrier_semaphore()
    for across in range(sides):
        for step in range(shards):
            if across or step:
                pl.semaphore_signal(
                    barrier,
                    inc=1,
                    device_id=(lax.rem(side + across, sides), lax.rem(seat + step, shards)),
                    device_id_type=MESH,
                )
    pl.semaphore_wait(barrier, sides * shards - 1)


def bring_kernel(
    plan, qk_ref, values_ref, place_ref, tokens_ref, places_ref,
    own_sem, line_send, line_recv, far_send, far_recv, near_send, near_recv, put_send, put_recv,
):
    sides, shards, heads, fars, nears = plan
    group = fars * nears
    side, seat = lax.axis_index("round"), lax.axis_index("seq")
    level, lane = seat // group, lax.rem(seat, group)
    far, near = lane // nears, lax.rem(lane, nears)

    def columns(head):
        return pl.ds(pl.multiple_of((side * heads + head) * HEAD_DIM, HEAD_DIM), HEAD_DIM)

    def seat_of(level, far, near):
        return level * group + far * nears + near

    def block_of(level, far, near):
        return (far * nears + near) * heads + level

    def remote(source, target, send, recv, to):
        return pltpu.make_async_remote_copy(
            src_ref=source, dst_ref=target, send_sem=send, recv_sem=recv,
            device_id=(side, to), device_id_type=MESH,
        )

    fields = (qk_ref, values_ref)
    mine = block_of(level, far, near)
    own = [
        pltpu.make_async_copy(fields[k].at[:, columns(level)], tokens_ref.at[mine, k], own_sem.at[k])
        for k in range(2)
    ]
    for copy in own:
        copy.start()
    greet_all(sides, shards, side, seat)

    sent = []
    line = {}
    for k in range(2):
        for step in near_first(heads):
            to = lax.rem(level + step, heads)
            copy = remote(
                fields[k].at[:, columns(to)], tokens_ref.at[mine, k],
                line_send.at[step - 1, k], line_recv.at[step - 1, k], seat_of(to, far, near),
            )
            copy.start()
            sent.append(copy)
            line[step, k] = copy

    puts = []
    for across in range(sides):
        for step in range(heads):
            for turn in range(nears):
                at = (across * heads + step) * nears + turn
                to = seat_of(lax.rem(level + step, heads), side, lax.rem(near + turn, nears))
                copy = pltpu.make_async_remote_copy(
                    src_ref=place_ref, dst_ref=places_ref.at[mine],
                    send_sem=put_send.at[at], recv_sem=put_recv.at[mine],
                    device_id=(lax.rem(side + across, sides), to), device_id_type=MESH,
                )
                puts.append(copy)
                if at:
                    copy.start()
    stays = pltpu.make_async_copy(place_ref, places_ref.at[mine], put_recv.at[mine])
    pl.when(far != side)(puts[0].start)
    pl.when(far == side)(stays.start)

    def pass_near(block, k, index):
        for turn in range(1, nears):
            copy = remote(
                tokens_ref.at[block, k], tokens_ref.at[block, k],
                near_send.at[turn - 1, index, k], near_recv.at[turn - 1, index, k],
                seat_of(level, far, lax.rem(near + turn, nears)),
            )
            copy.start()
            sent.append(copy)

    def pass_far(block, k, step):
        for turn in range(1, fars):
            copy = remote(
                tokens_ref.at[block, k], tokens_ref.at[block, k],
                far_send.at[turn - 1, step, k], far_recv.at[turn - 1, step, k],
                seat_of(level, lax.rem(far + turn, fars), near),
            )
            copy.start()
            sent.append(copy)

    def from_far(k, step):
        for turn in range(1, fars):
            source = block_of(
                lax.rem(level + heads - step, heads), lax.rem(far + fars - turn, fars), near
            )
            remote(
                tokens_ref.at[source, k], tokens_ref.at[source, k],
                far_send.at[turn - 1, step, k], far_recv.at[turn - 1, step, k], seat,
            ).wait_recv()
            pass_near(source, k, turn * heads + step)

    order = [(step, k) for k in range(2) for step in near_first(heads)]
    for k in range(2):
        own[k].wait()
        pass_far(mine, k, 0)
        pass_near(mine, k, 0)
    late = [(0, 0), (0, 1)]
    for step, k in order:
        source = block_of(lax.rem(level + heads - step, heads), far, near)
        line[step, k].wait_recv()
        pass_far(source, k, step)
        pass_near(source, k, step)
        from_far(late[0][1], late[0][0])
        late = late[1:] + [(step, k)]
    for step, k in late:
        from_far(k, step)
    for turn in range(1, nears):
        for away in range(fars):
            for step in range(heads):
                for k in range(2):
                    source = block_of(
                        lax.rem(level + heads - step, heads),
                        lax.rem(far + fars - away, fars),
                        lax.rem(near + nears - turn, nears),
                    )
                    index = away * heads + step
                    remote(
                        tokens_ref.at[source, k], tokens_ref.at[source, k],
                        near_send.at[turn - 1, index, k], near_recv.at[turn - 1, index, k], seat,
                    ).wait_recv()
    for block in range(shards):
        pltpu.make_async_copy(place_ref, places_ref.at[block], put_recv.at[block]).wait()
    for copy in sent:
        copy.wait_send()
    for copy in puts[1:]:
        copy.wait_send()
    pl.when(far != side)(puts[0].wait_send)


def bring_in(qk, values, place, plan):
    sides, shards, heads, fars, nears = plan
    rows = qk.shape[0]
    dma = pltpu.SemaphoreType.DMA
    return pl.pallas_call(
        functools.partial(bring_kernel, plan),
        out_shape=(
            jax.ShapeDtypeStruct((shards, 2, rows, HEAD_DIM), jnp.bfloat16),
            jax.ShapeDtypeStruct((shards,) + place.shape, jnp.int32),
        ),
        in_specs=[pl.BlockSpec(memory_space=pltpu.VMEM)] * 3,
        out_specs=(pl.BlockSpec(memory_space=pl.ANY), pl.BlockSpec(memory_space=pl.ANY)),
        scratch_shapes=[
            dma((2,)),
            dma((heads - 1, 2)),
            dma((heads - 1, 2)),
            dma((fars - 1, heads, 2)),
            dma((fars - 1, heads, 2)),
            dma((nears - 1, fars * heads, 2)),
            dma((nears - 1, fars * heads, 2)),
            dma((sides * heads * nears,)),
            dma((shards,)),
        ],
        compiler_params=pltpu.CompilerParams(
            collective_id=0, has_side_effects=True, vmem_limit_bytes=16 * 1024 * 1024
        ),
        name="bring_in",
    )(qk, values, place)


def head_groups(shards, heads):
    group = shards // heads
    along = [[lane + group * step for step in range(heads)] for lane in range(group)]
    within = [[group * step + lane for lane in range(group)] for step in range(heads)]
    return group, along, within


def slots_of(place, section, base, total):
    bound = section + STRETCH
    put = jnp.minimum(lax.rem(place - base + STRETCH + total, total), bound)
    take = jnp.where(put < STRETCH, bound, put)
    return put, take


def by_heads_on_device(qk, values, dest_dev, dest_slot):
    shards = lax.axis_size("seq")
    sides = lax.axis_size("round")
    rows, width = qk.shape
    heads = width // HEAD_DIM // sides
    total = rows * shards
    group, along, within = head_groups(shards, heads)
    parts = group // sides
    section = total // parts
    lane = lax.rem(lax.axis_index("seq"), group)
    place = dest_dev[0] * rows + dest_slot[0]
    plan = (sides, shards, heads, sides, parts)
    tokens, places = bring_in(qk, values, place.reshape(-1, HEAD_DIM), plan)
    put, take = slots_of(places.reshape(-1), section, lax.rem(lane, parts) * section, total)
    out, lse = local_attend(put, take, tokens, section)
    out = lax.all_to_all(
        out, "seq", split_axis=0, concat_axis=0, tiled=True, axis_index_groups=within
    ).reshape(group, heads, rows, HEAD_DIM)
    lse = lax.all_to_all(
        lse, "seq", split_axis=0, concat_axis=0, tiled=True, axis_index_groups=within
    ).reshape(group, heads, rows)
    weight = jnp.exp(lse - jnp.max(lse, axis=0, keepdims=True))
    weight = weight / jnp.sum(weight, axis=0, keepdims=True)
    merged = jnp.sum(weight[..., None] * out.astype(jnp.float32), axis=0).astype(jnp.bfloat16)
    merged = lax.all_to_all(
        merged, "seq", split_axis=0, concat_axis=0, tiled=True, axis_index_groups=along
    )
    return jnp.transpose(merged, (1, 0, 2)).reshape(rows, heads * HEAD_DIM)


def whole_head_fits(qk, shards, sides):
    rows, width = qk.shape
    heads = width // HEAD_DIM // sides
    bytes_held = rows * HEAD_DIM * shards * 2 * 2
    if shards % heads or (shards // heads) % sides:
        return False
    parts = shards // heads // sides
    if (rows * shards) % (parts * STRETCH) or parts < 2:
        return False
    return bytes_held <= 8 * 1024 * 1024


def either_plan(qk, values, dest_dev, dest_slot):
    if whole_head_fits(qk, lax.axis_size("seq"), lax.axis_size("round")):
        return by_heads_on_device(qk, values, dest_dev, dest_slot)
    return on_device(qk, values, dest_dev, dest_slot)


def solution(mesh):
    return jax.shard_map(
        either_plan,
        mesh=mesh,
        in_specs=(P("seq", None), P("seq", None), P("round", "seq"), P("round", "seq")),
        out_specs=P("seq", "round"),
        check_vma=False,
    )
```

```python
import functools

import jax
import jax.numpy as jnp
from jax import lax
from jax.experimental import pallas as pl
from jax.experimental.pallas import tpu as pltpu
from jax.sharding import PartitionSpec as P

HEAD_DIM = 128
STRETCH = 512


eps_norm = 1e-06
self_score = -100000.0


def passed_along(value, axis, steps):
    count = lax.axis_size(axis)
    pairs = [(source, (source + steps) % count) for source in range(count)]
    return lax.ppermute(value, axis, pairs)


def as_sent(array):
    return jax.tree.map(lambda a: a.astype(jnp.bfloat16) if a.dtype == jnp.float32 else a, array)


def unit_keys(rows):
    count = rows.shape[0]
    heads = rows.shape[1] // HEAD_DIM
    field = rows.astype(jnp.float32).reshape(count, heads, HEAD_DIM)
    field = field * lax.rsqrt(jnp.sum(field * field, axis=-1, keepdims=True) + eps_norm)
    return field.reshape(count, heads * HEAD_DIM).astype(jnp.bfloat16)


def spread_heads(weights):
    return jnp.repeat(weights, HEAD_DIM, axis=1)


def pack_round(qk, values, dest, slot, shards, cap):
    rows = qk.shape[0]
    hits = (dest[:, None] == jnp.arange(shards, dtype=jnp.int32)[None, :]).astype(jnp.int32)
    ranks = jnp.sum(hits * jnp.cumsum(hits, axis=0), axis=1) - 1
    position = dest * cap + ranks
    total = shards * cap
    send_qk = jnp.zeros((total, qk.shape[1]), qk.dtype).at[position].set(qk)
    send_values = jnp.zeros((total, values.shape[1]), values.dtype).at[position].set(values)
    send_slot = jnp.full((total,), rows, jnp.int32).at[position].set(slot)
    send_source = (
        jnp.full((total,), rows, jnp.int32).at[position].set(jnp.arange(rows, dtype=jnp.int32))
    )
    return (send_qk, send_values, send_slot, send_source)


def group_attend(queries, keys, vals):
    rows = queries.shape[0]
    heads = queries.shape[1] // HEAD_DIM
    qpart = queries.reshape(rows, heads, HEAD_DIM)
    kpart = keys.reshape(2 * rows, heads, HEAD_DIM)
    vpart = vals.reshape(2 * rows, heads, HEAD_DIM)
    scores = jnp.einsum("qhd,khd->hqk", qpart, kpart, preferred_element_type=jnp.float32)
    itself = (
        jnp.arange(2 * rows, dtype=jnp.int32)[None, :]
        == jnp.arange(rows, dtype=jnp.int32)[:, None] + rows
    )
    scores = jnp.where(itself[None], jnp.float32(self_score), scores)
    highest = jnp.max(scores, axis=-1)
    lse = highest + jnp.log(jnp.sum(jnp.exp(scores - highest[..., None]), axis=-1))
    probs = jnp.exp(scores - lse[..., None]).astype(jnp.bfloat16)
    attended = jnp.einsum("hqk,khd->qhd", probs, vpart, preferred_element_type=jnp.float32)
    return (attended.reshape(rows, heads * HEAD_DIM).astype(jnp.bfloat16), jnp.transpose(lse))


def attend_sorted(sorted_qk, sorted_values):
    rows = sorted_qk.shape[0]
    width = sorted_qk.shape[1]
    keys = unit_keys(sorted_qk)
    before_keys, before_values = passed_along((keys, sorted_values), "seq", 1)
    ext_keys = jnp.concatenate([before_keys, keys], axis=0)
    ext_values = jnp.concatenate([before_values, sorted_values], axis=0)
    group_width = width // 2

    def one_stretch(position):
        pieces = []
        totals = []
        for group in range(2):
            low = group * group_width
            high = low + group_width
            piece, total = group_attend(
                sorted_qk[:, low:high], ext_keys[:, low:high], ext_values[:, low:high]
            )
            pieces.append(piece)
            totals.append(total)
        return (jnp.concatenate(pieces, axis=1), jnp.concatenate(totals, axis=1))

    attended, lse = lax.map(one_stretch, jnp.arange(rows // STRETCH, dtype=jnp.int32))
    return (attended.reshape(rows, width), lse.reshape(rows, lse.shape[-1]))


def on_device(qk, values, dest_dev, dest_slot):
    shards = lax.axis_size("seq")
    rows = qk.shape[0]
    width = qk.shape[1]
    heads = width // HEAD_DIM
    cap = 3 * (rows // (2 * shards))
    send_qk, send_values, send_slot, send_source = pack_round(
        qk, values, dest_dev[0], dest_slot[0], shards, cap
    )
    got_qk, got_values, got_slot, got_source = (
        lax.all_to_all(send_qk, "seq", split_axis=0, concat_axis=0, tiled=True),
        lax.all_to_all(send_values, "seq", split_axis=0, concat_axis=0, tiled=True),
        lax.all_to_all(send_slot, "seq", split_axis=0, concat_axis=0, tiled=True),
        lax.all_to_all(send_source, "seq", split_axis=0, concat_axis=0, tiled=True),
    )
    sorted_qk = jnp.zeros((rows, width), jnp.bfloat16).at[got_slot].set(got_qk, mode="drop")
    sorted_values = jnp.zeros((rows, width), jnp.bfloat16).at[got_slot].set(got_values, mode="drop")
    attended, lse = attend_sorted(sorted_qk, sorted_values)
    lse = lse.reshape(rows, heads)
    picked = jnp.clip(got_slot, 0, rows - 1)
    reply_out = attended[picked]
    reply_lse = lse[picked]
    back_out, back_lse, back_ids = (
        lax.all_to_all(as_sent(reply_out), "seq", split_axis=0, concat_axis=0, tiled=True).astype(
            reply_out.dtype
        ),
        lax.all_to_all(as_sent(reply_lse), "seq", split_axis=0, concat_axis=0, tiled=True).astype(
            reply_lse.dtype
        ),
        lax.all_to_all(got_source, "seq", split_axis=0, concat_axis=0, tiled=True),
    )
    round_out = jnp.zeros((rows, width), jnp.bfloat16).at[back_ids].set(back_out, mode="drop")
    round_lse = jnp.zeros((rows, heads), jnp.float32).at[back_ids].set(back_lse, mode="drop")
    local_top = round_lse
    local_top = lax.pmax(local_top, "round")
    denom = jnp.exp(round_lse - local_top)
    numer = spread_heads(denom) * round_out.astype(jnp.float32)
    numer_half, denom_half = (
        lax.psum_scatter(
            numer.astype(jnp.bfloat16), "round", scatter_dimension=1, tiled=True
        ).astype(jnp.float32),
        lax.psum_scatter(
            denom.astype(jnp.bfloat16), "round", scatter_dimension=1, tiled=True
        ).astype(jnp.float32),
    )
    merged = numer_half / spread_heads(denom_half)
    return merged.astype(jnp.bfloat16)


NO_ROW = -1e30
CHUNK = 16


def local_kernel(
    put_ref, take_ref, tokens_ref, out_ref, lse_ref, wide_q, wide_v, sorted_q, sorted_v, att, logs
):
    blocks, _, rows, _ = tokens_ref.shape
    bound = sorted_q.shape[0] - 8

    @pl.loop(0, blocks)
    def _(block):
        wide_q[...] = tokens_ref[block, 0].astype(jnp.float32)
        wide_v[...] = tokens_ref[block, 1].astype(jnp.float32)

        @pl.loop(0, rows, step=CHUNK)
        def _(start):
            for row in range(CHUNK):
                to = put_ref[block * rows + start + row]
                sorted_q[pl.ds(to, 1), :] = wide_q[pl.ds(start + row, 1), :]
                sorted_v[pl.ds(to, 1), :] = wide_v[pl.ds(start + row, 1), :]

    att[pl.ds(bound, 8), :] = jnp.zeros((8, HEAD_DIM), jnp.float32)
    logs[pl.ds(bound, 8), :] = jnp.full((8, HEAD_DIM), NO_ROW, jnp.float32)

    @pl.loop(0, bound // STRETCH - 1)
    def _(stretch):
        low = pl.multiple_of(stretch * STRETCH, STRETCH)
        own = pl.multiple_of(low + STRETCH, STRETCH)
        queries = sorted_q[pl.ds(own, STRETCH), :].astype(jnp.bfloat16)
        field = sorted_q[pl.ds(low, 2 * STRETCH), :]
        scale = lax.rsqrt(jnp.sum(field * field, axis=-1, keepdims=True) + eps_norm)
        keys = (field * scale).astype(jnp.bfloat16)
        vals = sorted_v[pl.ds(low, 2 * STRETCH), :].astype(jnp.bfloat16)
        scores = lax.dot_general(
            queries, keys, (((1,), (1,)), ((), ())), preferred_element_type=jnp.float32
        )
        row_at = lax.broadcasted_iota(jnp.int32, scores.shape, 0) + STRETCH
        col_at = lax.broadcasted_iota(jnp.int32, scores.shape, 1)
        scores = jnp.where(row_at == col_at, jnp.float32(self_score), scores)
        highest = jnp.max(scores, axis=-1, keepdims=True)
        probs = jnp.exp(scores - highest)
        weight = jnp.sum(probs, axis=-1, keepdims=True)
        attended = jnp.dot(probs.astype(jnp.bfloat16), vals, preferred_element_type=jnp.float32)
        att[pl.ds(own, STRETCH), :] = attended / weight
        logs[pl.ds(own, STRETCH), :] = jnp.broadcast_to(
            highest + jnp.log(weight), (STRETCH, HEAD_DIM)
        )

    @pl.loop(0, blocks)
    def _(block):
        @pl.loop(0, rows, step=CHUNK)
        def _(start):
            for row in range(CHUNK):
                at = take_ref[block * rows + start + row]
                wide_q[pl.ds(start + row, 1), :] = att[pl.ds(at, 1), :]
                wide_v[pl.ds(start + row, 1), :] = logs[pl.ds(at, 1), :]

        out_ref[block] = wide_q[...].astype(jnp.bfloat16)
        lse_ref[block] = jnp.transpose(wide_v[...])[0:1, :]


def local_attend(put, take, tokens, section):
    blocks, _, rows, wide = tokens.shape
    bound = section + STRETCH + 8
    return pl.pallas_call(
        local_kernel,
        out_shape=(
            jax.ShapeDtypeStruct((blocks, rows, wide), jnp.bfloat16),
            jax.ShapeDtypeStruct((blocks, 1, rows), jnp.float32),
        ),
        in_specs=[
            pl.BlockSpec(memory_space=pltpu.SMEM),
            pl.BlockSpec(memory_space=pltpu.SMEM),
            pl.BlockSpec(memory_space=pltpu.VMEM),
        ],
        out_specs=(
            pl.BlockSpec(memory_space=pltpu.VMEM),
            pl.BlockSpec(memory_space=pltpu.VMEM),
        ),
        scratch_shapes=[
            pltpu.VMEM((rows, wide), jnp.float32),
            pltpu.VMEM((rows, wide), jnp.float32),
            pltpu.VMEM((bound, wide), jnp.float32),
            pltpu.VMEM((bound, wide), jnp.float32),
            pltpu.VMEM((bound, wide), jnp.float32),
            pltpu.VMEM((bound, wide), jnp.float32),
        ],
        compiler_params=pltpu.CompilerParams(vmem_limit_bytes=24 * 1024 * 1024),
        name="local_attend",
    )(put, take, tokens)


MESH = pl.DeviceIdType.MESH


def near_first(count):
    return sorted(range(1, count), key=lambda step: min(step, count - step))


def greet_all(sides, shards, side, seat):
    barrier = pltpu.get_barrier_semaphore()
    for across in range(sides):
        for step in range(shards):
            if across or step:
                pl.semaphore_signal(
                    barrier,
                    inc=1,
                    device_id=(lax.rem(side + across, sides), lax.rem(seat + step, shards)),
                    device_id_type=MESH,
                )
    pl.semaphore_wait(barrier, sides * shards - 1)


def bring_kernel(
    plan, qk_ref, values_ref, place_ref, tokens_ref, places_ref,
    own_sem, line_send, line_recv, far_send, far_recv, near_send, near_recv, put_send, put_recv,
):
    sides, shards, heads, fars, nears = plan
    group = fars * nears
    side, seat = lax.axis_index("round"), lax.axis_index("seq")
    level, lane = seat // group, lax.rem(seat, group)
    far, near = lane // nears, lax.rem(lane, nears)

    def columns(head):
        return pl.ds(pl.multiple_of((side * heads + head) * HEAD_DIM, HEAD_DIM), HEAD_DIM)

    def seat_of(level, far, near):
        return level * group + far * nears + near

    def block_of(level, far, near):
        return (far * nears + near) * heads + level

    def remote(source, target, send, recv, to):
        return pltpu.make_async_remote_copy(
            src_ref=source, dst_ref=target, send_sem=send, recv_sem=recv,
            device_id=(side, to), device_id_type=MESH,
        )

    fields = (qk_ref, values_ref)
    mine = block_of(level, far, near)
    own = [
        pltpu.make_async_copy(fields[k].at[:, columns(level)], tokens_ref.at[mine, k], own_sem.at[k])
        for k in range(2)
    ]
    for copy in own:
        copy.start()
    greet_all(sides, shards, side, seat)

    sent = []
    line = {}
    for k in range(2):
        for step in near_first(heads):
            to = lax.rem(level + step, heads)
            copy = remote(
                fields[k].at[:, columns(to)], tokens_ref.at[mine, k],
                line_send.at[step - 1, k], line_recv.at[step - 1, k], seat_of(to, far, near),
            )
            copy.start()
            sent.append(copy)
            line[step, k] = copy

    puts = []
    for across in range(sides):
        for step in range(heads):
            for turn in range(nears):
                at = (across * heads + step) * nears + turn
                to = seat_of(lax.rem(level + step, heads), side, lax.rem(near + turn, nears))
                copy = pltpu.make_async_remote_copy(
                    src_ref=place_ref, dst_ref=places_ref.at[mine],
                    send_sem=put_send.at[at], recv_sem=put_recv.at[mine],
                    device_id=(lax.rem(side + across, sides), to), device_id_type=MESH,
                )
                puts.append(copy)
                if at:
                    copy.start()
    stays = pltpu.make_async_copy(place_ref, places_ref.at[mine], put_recv.at[mine])
    pl.when(far != side)(puts[0].start)
    pl.when(far == side)(stays.start)

    def pass_near(block, k, index):
        for turn in range(1, nears):
            copy = remote(
                tokens_ref.at[block, k], tokens_ref.at[block, k],
                near_send.at[turn - 1, index, k], near_recv.at[turn - 1, index, k],
                seat_of(level, far, lax.rem(near + turn, nears)),
            )
            copy.start()
            sent.append(copy)

    def pass_far(block, k, step):
        for turn in range(1, fars):
            copy = remote(
                tokens_ref.at[block, k], tokens_ref.at[block, k],
                far_send.at[turn - 1, step, k], far_recv.at[turn - 1, step, k],
                seat_of(level, lax.rem(far + turn, fars), near),
            )
            copy.start()
            sent.append(copy)

    def from_far(k, step):
        for turn in range(1, fars):
            source = block_of(
                lax.rem(level + heads - step, heads), lax.rem(far + fars - turn, fars), near
            )
            remote(
                tokens_ref.at[source, k], tokens_ref.at[source, k],
                far_send.at[turn - 1, step, k], far_recv.at[turn - 1, step, k], seat,
            ).wait_recv()
            pass_near(source, k, turn * heads + step)

    order = [(step, k) for k in range(2) for step in near_first(heads)]
    for k in range(2):
        own[k].wait()
        pass_far(mine, k, 0)
        pass_near(mine, k, 0)
    late = [(0, 0), (0, 1)]
    for step, k in order:
        source = block_of(lax.rem(level + heads - step, heads), far, near)
        line[step, k].wait_recv()
        pass_far(source, k, step)
        pass_near(source, k, step)
        from_far(late[0][1], late[0][0])
        late = late[1:] + [(step, k)]
    for step, k in late:
        from_far(k, step)
    for turn in range(1, nears):
        for away in range(fars):
            for step in range(heads):
                for k in range(2):
                    source = block_of(
                        lax.rem(level + heads - step, heads),
                        lax.rem(far + fars - away, fars),
                        lax.rem(near + nears - turn, nears),
                    )
                    index = away * heads + step
                    remote(
                        tokens_ref.at[source, k], tokens_ref.at[source, k],
                        near_send.at[turn - 1, index, k], near_recv.at[turn - 1, index, k], seat,
                    ).wait_recv()
    for block in range(shards):
        pltpu.make_async_copy(place_ref, places_ref.at[block], put_recv.at[block]).wait()
    for copy in sent:
        copy.wait_send()
    for copy in puts[1:]:
        copy.wait_send()
    pl.when(far != side)(puts[0].wait_send)


def bring_in(qk, values, place, plan):
    sides, shards, heads, fars, nears = plan
    rows = qk.shape[0]
    dma = pltpu.SemaphoreType.DMA
    return pl.pallas_call(
        functools.partial(bring_kernel, plan),
        out_shape=(
            jax.ShapeDtypeStruct((shards, 2, rows, HEAD_DIM), jnp.bfloat16),
            jax.ShapeDtypeStruct((shards,) + place.shape, jnp.int32),
        ),
        in_specs=[pl.BlockSpec(memory_space=pltpu.VMEM)] * 3,
        out_specs=(pl.BlockSpec(memory_space=pl.ANY), pl.BlockSpec(memory_space=pl.ANY)),
        scratch_shapes=[
            dma((2,)),
            dma((heads - 1, 2)),
            dma((heads - 1, 2)),
            dma((fars - 1, heads, 2)),
            dma((fars - 1, heads, 2)),
            dma((nears - 1, fars * heads, 2)),
            dma((nears - 1, fars * heads, 2)),
            dma((sides * heads * nears,)),
            dma((shards,)),
        ],
        compiler_params=pltpu.CompilerParams(
            collective_id=0, has_side_effects=True, vmem_limit_bytes=16 * 1024 * 1024
        ),
        name="bring_in",
    )(qk, values, place)


def send_kernel(
    plan, part_ref, logs_ref, out_ref,
    near_part, near_logs, far_part, far_logs, pass_part, pass_logs, done,
    near_send, near_recv, near_log_send, near_log_recv,
    far_send, far_recv, far_log_send, far_log_recv, line_send, line_recv,
):
    sides, shards, heads, fars, nears = plan
    group = fars * nears
    side, seat = lax.axis_index("round"), lax.axis_index("seq")
    level, lane = seat // group, lax.rem(seat, group)
    far, near = lane // nears, lax.rem(lane, nears)
    rows = part_ref.shape[1]

    def seat_of(level, far, near):
        return level * group + far * nears + near

    def block_of(level, far, near):
        return (far * nears + near) * heads + level

    def remote(source, target, send, recv, to):
        return pltpu.make_async_remote_copy(
            src_ref=source, dst_ref=target, send_sem=send, recv_sem=recv,
            device_id=(side, to), device_id_type=MESH,
        )

    greet_all(sides, shards, side, seat)
    steps = near_first(heads)[::-1] + [0]
    aways = list(range(1, fars)) + [0]
    sent = []
    from_near, log_from_near = {}, {}
    for away in aways:
        for turn in range(1, nears):
            to_near = lax.rem(near + turn, nears)
            to = seat_of(level, far, to_near)
            copy = remote(
                logs_ref.at[pl.ds(block_of(0, lax.rem(far + away, fars), to_near), heads)],
                near_logs.at[turn - 1, away],
                near_log_send.at[turn - 1, away], near_log_recv.at[turn - 1, away], to,
            )
            copy.start()
            sent.append(copy)
            log_from_near[turn, away] = copy
    for away in aways:
        for step in steps:
            for turn in range(1, nears):
                to_near = lax.rem(near + turn, nears)
                at = away * heads + step
                copy = remote(
                    part_ref.at[
                        block_of(lax.rem(level + step, heads), lax.rem(far + away, fars), to_near)
                    ],
                    near_part.at[turn - 1, at],
                    near_send.at[turn - 1, at], near_recv.at[turn - 1, at],
                    seat_of(level, far, to_near),
                )
                copy.start()
                sent.append(copy)
                from_near[turn, at] = copy

    def logs_here(away):
        first = block_of(0, lax.rem(far + away, fars), near)
        total = logs_ref[pl.ds(first, heads)]
        for turn in range(1, nears):
            log_from_near[turn, away].wait_recv()
            total = jnp.maximum(total, near_logs[turn - 1, away])
        return total

    def part_here(away, step):
        at = away * heads + step
        total = part_ref[
            block_of(lax.rem(level + step, heads), lax.rem(far + away, fars), near)
        ].astype(jnp.float32)
        for turn in range(1, nears):
            from_near[turn, at].wait_recv()
            total = total + near_part[turn - 1, at].astype(jnp.float32)
        return total

    from_far, log_from_far = {}, {}
    for away in range(1, fars):
        pass_logs[away] = logs_here(away)
        copy = remote(
            pass_logs.at[away], far_logs.at[away - 1],
            far_log_send.at[away - 1], far_log_recv.at[away - 1],
            seat_of(level, lax.rem(far + away, fars), near),
        )
        copy.start()
        sent.append(copy)
        log_from_far[away] = copy
    pass_logs[0] = logs_here(0)
    for away in range(1, fars):
        for step in steps:
            pass_part[away - 1, step] = part_here(away, step).astype(jnp.bfloat16)
            copy = remote(
                pass_part.at[away - 1, step], far_part.at[away - 1, step],
                far_send.at[away - 1, step], far_recv.at[away - 1, step],
                seat_of(level, lax.rem(far + away, fars), near),
            )
            copy.start()
            sent.append(copy)
            from_far[away, step] = copy

    for away in range(1, fars):
        log_from_far[away].wait_recv()

    def spread(weight):
        return jnp.transpose(jnp.broadcast_to(weight, (HEAD_DIM, rows)))

    from_line = []
    for step in steps:
        to = lax.rem(level + step, heads)
        logs = [pass_logs[0, to]] + [far_logs[away - 1, to] for away in range(1, fars)]
        highest = functools.reduce(jnp.maximum, logs)
        weights = [jnp.exp(log - highest) for log in logs]
        total = functools.reduce(jnp.add, weights)
        merged = spread(weights[0] / total) * part_here(0, step)
        for away in range(1, fars):
            share = spread(weights[away] / total)
            from_far[away, step].wait_recv()
            merged = merged + share * far_part[away - 1, step].astype(jnp.float32)
        columns = pl.ds(pl.multiple_of(level * HEAD_DIM, HEAD_DIM), HEAD_DIM)
        if step:
            done[step - 1] = merged.astype(jnp.bfloat16)
            copy = remote(
                done.at[step - 1], out_ref.at[:, columns],
                line_send.at[step - 1], line_recv.at[step - 1], seat_of(to, far, near),
            )
            copy.start()
            sent.append(copy)
            from_line.append(copy)
        else:
            out_ref[:, columns] = merged.astype(jnp.bfloat16)
    for copy in from_line:
        copy.wait_recv()
    for copy in sent:
        copy.wait_send()


def send_back(part, logs, plan):
    sides, shards, heads, fars, nears = plan
    rows = part.shape[1]
    dma = pltpu.SemaphoreType.DMA

    def held(*lead):
        return pltpu.VMEM(lead + (rows, HEAD_DIM), jnp.bfloat16)

    def logs_held(*lead):
        return pltpu.VMEM(lead + (heads, 1, rows), jnp.float32)

    near_shape, far_shape = (nears - 1, fars * heads), (fars - 1, heads)
    return pl.pallas_call(
        functools.partial(send_kernel, plan),
        out_shape=jax.ShapeDtypeStruct((rows, heads * HEAD_DIM), jnp.bfloat16),
        in_specs=[pl.BlockSpec(memory_space=pltpu.VMEM)] * 2,
        out_specs=pl.BlockSpec(memory_space=pltpu.VMEM),
        scratch_shapes=[
            held(*near_shape), logs_held(nears - 1, fars),
            held(*far_shape), logs_held(fars - 1),
            held(*far_shape), logs_held(fars),
            held(heads - 1),
            dma(near_shape), dma(near_shape), dma((nears - 1, fars)), dma((nears - 1, fars)),
            dma(far_shape), dma(far_shape), dma((fars - 1,)), dma((fars - 1,)),
            dma((heads - 1,)), dma((heads - 1,)),
        ],
        compiler_params=pltpu.CompilerParams(
            collective_id=1, has_side_effects=True, vmem_limit_bytes=24 * 1024 * 1024
        ),
        name="send_back",
    )(part, logs)


def slots_of(place, section, base, total):
    bound = section + STRETCH
    put = jnp.minimum(lax.rem(place - base + STRETCH + total, total), bound)
    take = jnp.where(put < STRETCH, bound, put)
    return put, take


def by_heads_on_device(qk, values, dest_dev, dest_slot):
    shards = lax.axis_size("seq")
    sides = lax.axis_size("round")
    rows, width = qk.shape
    heads = width // HEAD_DIM // sides
    total = rows * shards
    group = shards // heads
    parts = group // sides
    section = total // parts
    lane = lax.rem(lax.axis_index("seq"), group)
    place = dest_dev[0] * rows + dest_slot[0]
    plan = (sides, shards, heads, sides, parts)
    tokens, places = bring_in(qk, values, place.reshape(-1, HEAD_DIM), plan)
    put, take = slots_of(places.reshape(-1), section, lax.rem(lane, parts) * section, total)
    part, logs = local_attend(put, take, tokens, section)
    return send_back(part, logs, plan)


def whole_head_fits(qk, shards, sides):
    rows, width = qk.shape
    heads = width // HEAD_DIM // sides
    bytes_held = rows * HEAD_DIM * shards * 2 * 2
    if shards % heads or (shards // heads) % sides:
        return False
    parts = shards // heads // sides
    if (rows * shards) % (parts * STRETCH) or parts < 2:
        return False
    return bytes_held <= 8 * 1024 * 1024


def either_plan(qk, values, dest_dev, dest_slot):
    if whole_head_fits(qk, lax.axis_size("seq"), lax.axis_size("round")):
        return by_heads_on_device(qk, values, dest_dev, dest_slot)
    return on_device(qk, values, dest_dev, dest_slot)


def solution(mesh):
    return jax.shard_map(
        either_plan,
        mesh=mesh,
        in_specs=(P("seq", None), P("seq", None), P("round", "seq"), P("round", "seq")),
        out_specs=P("seq", "round"),
        check_vma=False,
    )
```

```python
import functools

import jax
import jax.numpy as jnp
from jax import lax
from jax.experimental import pallas as pl
from jax.experimental.pallas import tpu as pltpu
from jax.sharding import PartitionSpec as P

HEAD_DIM = 128
STRETCH = 512


eps_norm = 1e-06
self_score = -100000.0


def passed_along(value, axis, steps):
    count = lax.axis_size(axis)
    pairs = [(source, (source + steps) % count) for source in range(count)]
    return lax.ppermute(value, axis, pairs)


def as_sent(array):
    return jax.tree.map(lambda a: a.astype(jnp.bfloat16) if a.dtype == jnp.float32 else a, array)


def unit_keys(rows):
    count = rows.shape[0]
    heads = rows.shape[1] // HEAD_DIM
    field = rows.astype(jnp.float32).reshape(count, heads, HEAD_DIM)
    field = field * lax.rsqrt(jnp.sum(field * field, axis=-1, keepdims=True) + eps_norm)
    return field.reshape(count, heads * HEAD_DIM).astype(jnp.bfloat16)


def spread_heads(weights):
    return jnp.repeat(weights, HEAD_DIM, axis=1)


def pack_round(qk, values, dest, slot, shards, cap):
    rows = qk.shape[0]
    hits = (dest[:, None] == jnp.arange(shards, dtype=jnp.int32)[None, :]).astype(jnp.int32)
    ranks = jnp.sum(hits * jnp.cumsum(hits, axis=0), axis=1) - 1
    position = dest * cap + ranks
    total = shards * cap
    send_qk = jnp.zeros((total, qk.shape[1]), qk.dtype).at[position].set(qk)
    send_values = jnp.zeros((total, values.shape[1]), values.dtype).at[position].set(values)
    send_slot = jnp.full((total,), rows, jnp.int32).at[position].set(slot)
    send_source = (
        jnp.full((total,), rows, jnp.int32).at[position].set(jnp.arange(rows, dtype=jnp.int32))
    )
    return (send_qk, send_values, send_slot, send_source)


def group_attend(queries, keys, vals):
    rows = queries.shape[0]
    heads = queries.shape[1] // HEAD_DIM
    qpart = queries.reshape(rows, heads, HEAD_DIM)
    kpart = keys.reshape(2 * rows, heads, HEAD_DIM)
    vpart = vals.reshape(2 * rows, heads, HEAD_DIM)
    scores = jnp.einsum("qhd,khd->hqk", qpart, kpart, preferred_element_type=jnp.float32)
    itself = (
        jnp.arange(2 * rows, dtype=jnp.int32)[None, :]
        == jnp.arange(rows, dtype=jnp.int32)[:, None] + rows
    )
    scores = jnp.where(itself[None], jnp.float32(self_score), scores)
    highest = jnp.max(scores, axis=-1)
    lse = highest + jnp.log(jnp.sum(jnp.exp(scores - highest[..., None]), axis=-1))
    probs = jnp.exp(scores - lse[..., None]).astype(jnp.bfloat16)
    attended = jnp.einsum("hqk,khd->qhd", probs, vpart, preferred_element_type=jnp.float32)
    return (attended.reshape(rows, heads * HEAD_DIM).astype(jnp.bfloat16), jnp.transpose(lse))


def attend_sorted(sorted_qk, sorted_values):
    rows = sorted_qk.shape[0]
    width = sorted_qk.shape[1]
    keys = unit_keys(sorted_qk)
    before_keys, before_values = passed_along((keys, sorted_values), "seq", 1)
    ext_keys = jnp.concatenate([before_keys, keys], axis=0)
    ext_values = jnp.concatenate([before_values, sorted_values], axis=0)
    group_width = width // 2

    def one_stretch(position):
        pieces = []
        totals = []
        for group in range(2):
            low = group * group_width
            high = low + group_width
            piece, total = group_attend(
                sorted_qk[:, low:high], ext_keys[:, low:high], ext_values[:, low:high]
            )
            pieces.append(piece)
            totals.append(total)
        return (jnp.concatenate(pieces, axis=1), jnp.concatenate(totals, axis=1))

    attended, lse = lax.map(one_stretch, jnp.arange(rows // STRETCH, dtype=jnp.int32))
    return (attended.reshape(rows, width), lse.reshape(rows, lse.shape[-1]))


def on_device(qk, values, dest_dev, dest_slot):
    shards = lax.axis_size("seq")
    rows = qk.shape[0]
    width = qk.shape[1]
    heads = width // HEAD_DIM
    cap = 3 * (rows // (2 * shards))
    send_qk, send_values, send_slot, send_source = pack_round(
        qk, values, dest_dev[0], dest_slot[0], shards, cap
    )
    got_qk, got_values, got_slot, got_source = (
        lax.all_to_all(send_qk, "seq", split_axis=0, concat_axis=0, tiled=True),
        lax.all_to_all(send_values, "seq", split_axis=0, concat_axis=0, tiled=True),
        lax.all_to_all(send_slot, "seq", split_axis=0, concat_axis=0, tiled=True),
        lax.all_to_all(send_source, "seq", split_axis=0, concat_axis=0, tiled=True),
    )
    sorted_qk = jnp.zeros((rows, width), jnp.bfloat16).at[got_slot].set(got_qk, mode="drop")
    sorted_values = jnp.zeros((rows, width), jnp.bfloat16).at[got_slot].set(got_values, mode="drop")
    attended, lse = attend_sorted(sorted_qk, sorted_values)
    lse = lse.reshape(rows, heads)
    picked = jnp.clip(got_slot, 0, rows - 1)
    reply_out = attended[picked]
    reply_lse = lse[picked]
    back_out, back_lse, back_ids = (
        lax.all_to_all(as_sent(reply_out), "seq", split_axis=0, concat_axis=0, tiled=True).astype(
            reply_out.dtype
        ),
        lax.all_to_all(as_sent(reply_lse), "seq", split_axis=0, concat_axis=0, tiled=True).astype(
            reply_lse.dtype
        ),
        lax.all_to_all(got_source, "seq", split_axis=0, concat_axis=0, tiled=True),
    )
    round_out = jnp.zeros((rows, width), jnp.bfloat16).at[back_ids].set(back_out, mode="drop")
    round_lse = jnp.zeros((rows, heads), jnp.float32).at[back_ids].set(back_lse, mode="drop")
    local_top = round_lse
    local_top = lax.pmax(local_top, "round")
    denom = jnp.exp(round_lse - local_top)
    numer = spread_heads(denom) * round_out.astype(jnp.float32)
    numer_half, denom_half = (
        lax.psum_scatter(
            numer.astype(jnp.bfloat16), "round", scatter_dimension=1, tiled=True
        ).astype(jnp.float32),
        lax.psum_scatter(
            denom.astype(jnp.bfloat16), "round", scatter_dimension=1, tiled=True
        ).astype(jnp.float32),
    )
    merged = numer_half / spread_heads(denom_half)
    return merged.astype(jnp.bfloat16)


NO_ROW = -1e30
STRIP = 128


def local_kernel(put_ref, take_ref, tokens_ref, out_ref, lse_ref, wide, both, keys, vals):
    blocks, _, rows, _ = tokens_ref.shape
    bound = keys.shape[0]
    moves = put_ref.shape[1]
    pairs = rows // moves

    @pl.loop(0, blocks)
    def _(block):
        for k in range(2):
            wide[pl.ds(k, rows, stride=2), :] = tokens_ref[block, k].astype(jnp.float32)

        @pl.loop(0, pairs)
        def _(group):
            line = block * pairs + group
            start = pl.multiple_of(group * (2 * moves), 2 * moves)
            for row in range(moves):
                to = put_ref[line, row]
                both[pl.ds(to, 2), :] = wide[pl.ds(start + 2 * row, 2), :]

    @pl.loop(0, bound // STRETCH)
    def _(stretch):
        low = pl.multiple_of(stretch * STRETCH, STRETCH)
        field = both[pl.ds(2 * low, STRETCH, stride=2), :]
        scale = lax.rsqrt(jnp.sum(field * field, axis=-1, keepdims=True) + eps_norm)
        keys[pl.ds(low, STRETCH), :] = (field * scale).astype(jnp.bfloat16)
        vals[pl.ds(low, STRETCH), :HEAD_DIM] = both[
            pl.ds(2 * low + 1, STRETCH, stride=2), :
        ].astype(jnp.bfloat16)
        vals[pl.ds(low, STRETCH), HEAD_DIM:] = jnp.ones((STRETCH, HEAD_DIM), jnp.bfloat16)

    row_at = lax.broadcasted_iota(jnp.int32, (STRIP, STRIP), 0)
    col_at = lax.broadcasted_iota(jnp.int32, (STRIP, STRIP), 1)

    @pl.loop(0, bound // STRETCH - 1)
    def _(stretch):
        low = pl.multiple_of(stretch * STRETCH, STRETCH)
        window = keys[pl.ds(low, 2 * STRETCH), :]
        seen = vals[pl.ds(low, 2 * STRETCH), :]
        for strip in range(0, STRETCH, STRIP):
            at = 2 * (low + STRETCH + strip)
            queries = both[pl.ds(at, STRIP, stride=2), :].astype(jnp.bfloat16)
            scores = lax.dot_general(
                queries, window, (((1,), (1,)), ((), ())), preferred_element_type=jnp.float32
            )
            left, right = STRETCH + strip, STRETCH + strip + STRIP
            pieces = [
                scores[:, :left],
                jnp.where(row_at == col_at, jnp.float32(self_score), scores[:, left:right]),
            ]
            if right < 2 * STRETCH:
                pieces.append(scores[:, right:])
            scores = jnp.concatenate(pieces, axis=1)
            highest = jnp.max(scores, axis=-1, keepdims=True)
            probs = jnp.exp(scores - highest).astype(jnp.bfloat16)
            summed = jnp.dot(probs, seen, preferred_element_type=jnp.float32)
            weight = summed[:, HEAD_DIM:]
            both[pl.ds(at, STRIP, stride=2), :] = summed[:, :HEAD_DIM] / weight
            both[pl.ds(at + 1, STRIP, stride=2), :] = highest + jnp.log(weight)

    parity = lax.rem(lax.broadcasted_iota(jnp.int32, (8, HEAD_DIM), 0), 2)
    both[pl.ds(2 * bound, 8), :] = jnp.where(parity == 0, 0.0, NO_ROW).astype(jnp.float32)

    @pl.loop(0, blocks)
    def _(block):
        @pl.loop(0, pairs)
        def _(group):
            line = block * pairs + group
            start = pl.multiple_of(group * (2 * moves), 2 * moves)
            for row in range(moves):
                at = take_ref[line, row]
                wide[pl.ds(start + 2 * row, 2), :] = both[pl.ds(at, 2), :]

        out_ref[block] = wide[pl.ds(0, rows, stride=2), :].astype(jnp.bfloat16)
        lse_ref[block] = jnp.transpose(wide[pl.ds(1, rows, stride=2), :])[0:1, :]


def local_attend(put, take, tokens, section):
    blocks, _, rows, wide = tokens.shape
    bound = section + STRETCH
    return pl.pallas_call(
        local_kernel,
        out_shape=(
            jax.ShapeDtypeStruct((blocks, rows, wide), jnp.bfloat16),
            jax.ShapeDtypeStruct((blocks, 1, rows), jnp.float32),
        ),
        in_specs=[
            pl.BlockSpec(memory_space=pltpu.SMEM),
            pl.BlockSpec(memory_space=pltpu.SMEM),
            pl.BlockSpec(memory_space=pltpu.VMEM),
        ],
        out_specs=(
            pl.BlockSpec(memory_space=pltpu.VMEM),
            pl.BlockSpec(memory_space=pltpu.VMEM),
        ),
        scratch_shapes=[
            pltpu.VMEM((2 * rows, wide), jnp.float32),
            pltpu.VMEM((2 * bound + 8, wide), jnp.float32),
            pltpu.VMEM((bound, wide), jnp.bfloat16),
            pltpu.VMEM((bound, 2 * wide), jnp.bfloat16),
        ],
        compiler_params=pltpu.CompilerParams(vmem_limit_bytes=24 * 1024 * 1024),
        name="local_attend",
    )(put, take, tokens)


MESH = pl.DeviceIdType.MESH


def near_first(count):
    return sorted(range(1, count), key=lambda step: min(step, count - step))


def greet_all(sides, shards, side, seat):
    barrier = pltpu.get_barrier_semaphore()
    for across in range(sides):
        for step in range(shards):
            if across or step:
                pl.semaphore_signal(
                    barrier,
                    inc=1,
                    device_id=(lax.rem(side + across, sides), lax.rem(seat + step, shards)),
                    device_id_type=MESH,
                )
    pl.semaphore_wait(barrier, sides * shards - 1)


def bring_kernel(
    plan, qk_ref, values_ref, place_ref, tokens_ref, places_ref,
    own_sem, line_send, line_recv, far_send, far_recv, near_send, near_recv, put_send, put_recv,
):
    sides, shards, heads, fars, nears = plan
    group = fars * nears
    side, seat = lax.axis_index("round"), lax.axis_index("seq")
    level, lane = seat // group, lax.rem(seat, group)
    far, near = lane // nears, lax.rem(lane, nears)

    def columns(head):
        return pl.ds(pl.multiple_of((side * heads + head) * HEAD_DIM, HEAD_DIM), HEAD_DIM)

    def seat_of(level, far, near):
        return level * group + far * nears + near

    def block_of(level, far, near):
        return (far * nears + near) * heads + level

    def remote(source, target, send, recv, to):
        return pltpu.make_async_remote_copy(
            src_ref=source, dst_ref=target, send_sem=send, recv_sem=recv,
            device_id=(side, to), device_id_type=MESH,
        )

    fields = (qk_ref, values_ref)
    mine = block_of(level, far, near)
    own = [
        pltpu.make_async_copy(fields[k].at[:, columns(level)], tokens_ref.at[mine, k], own_sem.at[k])
        for k in range(2)
    ]
    for copy in own:
        copy.start()
    greet_all(sides, shards, side, seat)

    sent = []
    line = {}
    for k in range(2):
        for step in near_first(heads):
            to = lax.rem(level + step, heads)
            copy = remote(
                fields[k].at[:, columns(to)], tokens_ref.at[mine, k],
                line_send.at[step - 1, k], line_recv.at[step - 1, k], seat_of(to, far, near),
            )
            copy.start()
            sent.append(copy)
            line[step, k] = copy

    puts = []
    for across in range(sides):
        for step in range(heads):
            for turn in range(nears):
                at = (across * heads + step) * nears + turn
                to = seat_of(lax.rem(level + step, heads), side, lax.rem(near + turn, nears))
                copy = pltpu.make_async_remote_copy(
                    src_ref=place_ref, dst_ref=places_ref.at[mine],
                    send_sem=put_send.at[at], recv_sem=put_recv.at[mine],
                    device_id=(lax.rem(side + across, sides), to), device_id_type=MESH,
                )
                puts.append(copy)
                if at:
                    copy.start()
    stays = pltpu.make_async_copy(place_ref, places_ref.at[mine], put_recv.at[mine])
    pl.when(far != side)(puts[0].start)
    pl.when(far == side)(stays.start)

    def pass_near(block, k, index):
        for turn in range(1, nears):
            copy = remote(
                tokens_ref.at[block, k], tokens_ref.at[block, k],
                near_send.at[turn - 1, index, k], near_recv.at[turn - 1, index, k],
                seat_of(level, far, lax.rem(near + turn, nears)),
            )
            copy.start()
            sent.append(copy)

    def pass_far(block, k, step):
        for turn in range(1, fars):
            copy = remote(
                tokens_ref.at[block, k], tokens_ref.at[block, k],
                far_send.at[turn - 1, step, k], far_recv.at[turn - 1, step, k],
                seat_of(level, lax.rem(far + turn, fars), near),
            )
            copy.start()
            sent.append(copy)

    def from_far(k, step):
        for turn in range(1, fars):
            source = block_of(
                lax.rem(level + heads - step, heads), lax.rem(far + fars - turn, fars), near
            )
            remote(
                tokens_ref.at[source, k], tokens_ref.at[source, k],
                far_send.at[turn - 1, step, k], far_recv.at[turn - 1, step, k], seat,
            ).wait_recv()
            pass_near(source, k, turn * heads + step)

    order = [(step, k) for k in range(2) for step in near_first(heads)]
    for k in range(2):
        own[k].wait()
        pass_far(mine, k, 0)
        pass_near(mine, k, 0)
    late = [(0, 0), (0, 1)]
    for step, k in order:
        source = block_of(lax.rem(level + heads - step, heads), far, near)
        line[step, k].wait_recv()
        pass_far(source, k, step)
        pass_near(source, k, step)
        from_far(late[0][1], late[0][0])
        late = late[1:] + [(step, k)]
    for step, k in late:
        from_far(k, step)
    for turn in range(1, nears):
        for away in range(fars):
            for step in range(heads):
                for k in range(2):
                    source = block_of(
                        lax.rem(level + heads - step, heads),
                        lax.rem(far + fars - away, fars),
                        lax.rem(near + nears - turn, nears),
                    )
                    index = away * heads + step
                    remote(
                        tokens_ref.at[source, k], tokens_ref.at[source, k],
                        near_send.at[turn - 1, index, k], near_recv.at[turn - 1, index, k], seat,
                    ).wait_recv()
    for block in range(shards):
        pltpu.make_async_copy(place_ref, places_ref.at[block], put_recv.at[block]).wait()
    for copy in sent:
        copy.wait_send()
    for copy in puts[1:]:
        copy.wait_send()
    pl.when(far != side)(puts[0].wait_send)


def bring_in(qk, values, place, plan):
    sides, shards, heads, fars, nears = plan
    rows = qk.shape[0]
    dma = pltpu.SemaphoreType.DMA
    return pl.pallas_call(
        functools.partial(bring_kernel, plan),
        out_shape=(
            jax.ShapeDtypeStruct((shards, 2, rows, HEAD_DIM), jnp.bfloat16),
            jax.ShapeDtypeStruct((shards,) + place.shape, jnp.int32),
        ),
        in_specs=[pl.BlockSpec(memory_space=pltpu.HBM)] * 2 + [pl.BlockSpec(memory_space=pltpu.VMEM)],
        out_specs=(pl.BlockSpec(memory_space=pl.ANY), pl.BlockSpec(memory_space=pl.ANY)),
        scratch_shapes=[
            dma((2,)),
            dma((heads - 1, 2)),
            dma((heads - 1, 2)),
            dma((fars - 1, heads, 2)),
            dma((fars - 1, heads, 2)),
            dma((nears - 1, fars * heads, 2)),
            dma((nears - 1, fars * heads, 2)),
            dma((sides * heads * nears,)),
            dma((shards,)),
        ],
        compiler_params=pltpu.CompilerParams(
            collective_id=0, has_side_effects=True, vmem_limit_bytes=16 * 1024 * 1024
        ),
        name="bring_in",
    )(qk, values, place)


def send_kernel(
    plan, part_ref, logs_ref, out_ref,
    near_part, near_logs, far_part, far_logs, pass_part, pass_logs, done,
    near_send, near_recv, near_log_send, near_log_recv,
    far_send, far_recv, far_log_send, far_log_recv, line_send, line_recv,
):
    sides, shards, heads, fars, nears = plan
    group = fars * nears
    side, seat = lax.axis_index("round"), lax.axis_index("seq")
    level, lane = seat // group, lax.rem(seat, group)
    far, near = lane // nears, lax.rem(lane, nears)
    rows = part_ref.shape[1]

    def seat_of(level, far, near):
        return level * group + far * nears + near

    def block_of(level, far, near):
        return (far * nears + near) * heads + level

    def remote(source, target, send, recv, to):
        return pltpu.make_async_remote_copy(
            src_ref=source, dst_ref=target, send_sem=send, recv_sem=recv,
            device_id=(side, to), device_id_type=MESH,
        )

    greet_all(sides, shards, side, seat)
    steps = near_first(heads)[::-1] + [0]
    aways = list(range(1, fars)) + [0]
    sent = []
    from_near, log_from_near = {}, {}
    for away in aways:
        for turn in range(1, nears):
            to_near = lax.rem(near + turn, nears)
            to = seat_of(level, far, to_near)
            copy = remote(
                logs_ref.at[pl.ds(block_of(0, lax.rem(far + away, fars), to_near), heads)],
                near_logs.at[turn - 1, away],
                near_log_send.at[turn - 1, away], near_log_recv.at[turn - 1, away], to,
            )
            copy.start()
            sent.append(copy)
            log_from_near[turn, away] = copy
    for away in aways:
        for step in steps:
            for turn in range(1, nears):
                to_near = lax.rem(near + turn, nears)
                at = away * heads + step
                copy = remote(
                    part_ref.at[
                        block_of(lax.rem(level + step, heads), lax.rem(far + away, fars), to_near)
                    ],
                    near_part.at[turn - 1, at],
                    near_send.at[turn - 1, at], near_recv.at[turn - 1, at],
                    seat_of(level, far, to_near),
                )
                copy.start()
                sent.append(copy)
                from_near[turn, at] = copy

    def logs_here(away):
        first = block_of(0, lax.rem(far + away, fars), near)
        total = logs_ref[pl.ds(first, heads)]
        for turn in range(1, nears):
            log_from_near[turn, away].wait_recv()
            total = jnp.maximum(total, near_logs[turn - 1, away])
        return total

    def part_here(away, step):
        at = away * heads + step
        total = part_ref[
            block_of(lax.rem(level + step, heads), lax.rem(far + away, fars), near)
        ].astype(jnp.float32)
        for turn in range(1, nears):
            from_near[turn, at].wait_recv()
            total = total + near_part[turn - 1, at].astype(jnp.float32)
        return total

    from_far, log_from_far = {}, {}
    for away in range(1, fars):
        pass_logs[away] = logs_here(away)
        copy = remote(
            pass_logs.at[away], far_logs.at[away - 1],
            far_log_send.at[away - 1], far_log_recv.at[away - 1],
            seat_of(level, lax.rem(far + away, fars), near),
        )
        copy.start()
        sent.append(copy)
        log_from_far[away] = copy
    pass_logs[0] = logs_here(0)
    for away in range(1, fars):
        for step in steps:
            pass_part[away - 1, step] = part_here(away, step).astype(jnp.bfloat16)
            copy = remote(
                pass_part.at[away - 1, step], far_part.at[away - 1, step],
                far_send.at[away - 1, step], far_recv.at[away - 1, step],
                seat_of(level, lax.rem(far + away, fars), near),
            )
            copy.start()
            sent.append(copy)
            from_far[away, step] = copy

    for away in range(1, fars):
        log_from_far[away].wait_recv()

    def spread(weight):
        return jnp.transpose(jnp.broadcast_to(weight, (HEAD_DIM, rows)))

    from_line = []
    for step in steps:
        to = lax.rem(level + step, heads)
        logs = [pass_logs[0, to]] + [far_logs[away - 1, to] for away in range(1, fars)]
        highest = functools.reduce(jnp.maximum, logs)
        weights = [jnp.exp(log - highest) for log in logs]
        total = functools.reduce(jnp.add, weights)
        merged = spread(weights[0] / total) * part_here(0, step)
        for away in range(1, fars):
            share = spread(weights[away] / total)
            from_far[away, step].wait_recv()
            merged = merged + share * far_part[away - 1, step].astype(jnp.float32)
        columns = pl.ds(pl.multiple_of(level * HEAD_DIM, HEAD_DIM), HEAD_DIM)
        if step:
            done[step - 1] = merged.astype(jnp.bfloat16)
            copy = remote(
                done.at[step - 1], out_ref.at[:, columns],
                line_send.at[step - 1], line_recv.at[step - 1], seat_of(to, far, near),
            )
            copy.start()
            sent.append(copy)
            from_line.append(copy)
        else:
            out_ref[:, columns] = merged.astype(jnp.bfloat16)
    for copy in from_line:
        copy.wait_recv()
    for copy in sent:
        copy.wait_send()


def send_back(part, logs, plan):
    sides, shards, heads, fars, nears = plan
    rows = part.shape[1]
    dma = pltpu.SemaphoreType.DMA

    def held(*lead):
        return pltpu.VMEM(lead + (rows, HEAD_DIM), jnp.bfloat16)

    def logs_held(*lead):
        return pltpu.VMEM(lead + (heads, 1, rows), jnp.float32)

    near_shape, far_shape = (nears - 1, fars * heads), (fars - 1, heads)
    return pl.pallas_call(
        functools.partial(send_kernel, plan),
        out_shape=jax.ShapeDtypeStruct((rows, heads * HEAD_DIM), jnp.bfloat16),
        in_specs=[pl.BlockSpec(memory_space=pltpu.VMEM)] * 2,
        out_specs=pl.BlockSpec(memory_space=pltpu.VMEM),
        scratch_shapes=[
            held(*near_shape), logs_held(nears - 1, fars),
            held(*far_shape), logs_held(fars - 1),
            held(*far_shape), logs_held(fars),
            held(heads - 1),
            dma(near_shape), dma(near_shape), dma((nears - 1, fars)), dma((nears - 1, fars)),
            dma(far_shape), dma(far_shape), dma((fars - 1,)), dma((fars - 1,)),
            dma((heads - 1,)), dma((heads - 1,)),
        ],
        compiler_params=pltpu.CompilerParams(
            collective_id=1, has_side_effects=True, vmem_limit_bytes=24 * 1024 * 1024
        ),
        name="send_back",
    )(part, logs)


def slots_of(place, section, base, total):
    bound = section + STRETCH
    put = jnp.minimum(lax.rem(place - base + STRETCH + total, total), bound)
    take = jnp.where(put < STRETCH, bound, put)
    return 2 * put, 2 * take


def by_heads_on_device(qk, values, dest_dev, dest_slot):
    shards = lax.axis_size("seq")
    sides = lax.axis_size("round")
    rows, width = qk.shape
    heads = width // HEAD_DIM // sides
    total = rows * shards
    group = shards // heads
    parts = group // sides
    section = total // parts
    lane = lax.rem(lax.axis_index("seq"), group)
    place = dest_dev[0] * rows + dest_slot[0]
    plan = (sides, shards, heads, sides, parts)
    tokens, places = bring_in(qk, values, place.reshape(-1, HEAD_DIM), plan)
    put, take = slots_of(places.reshape(-1, HEAD_DIM), section, lax.rem(lane, parts) * section, total)
    part, logs = local_attend(put, take, tokens, section)
    return send_back(part, logs, plan)


def whole_head_fits(qk, shards, sides):
    rows, width = qk.shape
    heads = width // HEAD_DIM // sides
    bytes_held = rows * HEAD_DIM * shards * 2 * 2
    if shards % heads or (shards // heads) % sides:
        return False
    parts = shards // heads // sides
    if (rows * shards) % (parts * STRETCH) or parts < 2:
        return False
    return bytes_held <= 8 * 1024 * 1024


def either_plan(qk, values, dest_dev, dest_slot):
    if whole_head_fits(qk, lax.axis_size("seq"), lax.axis_size("round")):
        return by_heads_on_device(qk, values, dest_dev, dest_slot)
    return on_device(qk, values, dest_dev, dest_slot)


def solution(mesh):
    return jax.shard_map(
        either_plan,
        mesh=mesh,
        in_specs=(P("seq", None), P("seq", None), P("round", "seq"), P("round", "seq")),
        out_specs=P("seq", "round"),
        check_vma=False,
    )
```

```python
import functools

import jax
import jax.numpy as jnp
from jax import lax
from jax.experimental import pallas as pl
from jax.experimental.pallas import tpu as pltpu
from jax.sharding import PartitionSpec as P

HEAD_DIM = 128
STRETCH = 512


eps_norm = 1e-06
self_score = -100000.0


def passed_along(value, axis, steps):
    count = lax.axis_size(axis)
    pairs = [(source, (source + steps) % count) for source in range(count)]
    return lax.ppermute(value, axis, pairs)


def as_sent(array):
    return jax.tree.map(lambda a: a.astype(jnp.bfloat16) if a.dtype == jnp.float32 else a, array)


def unit_keys(rows):
    count = rows.shape[0]
    heads = rows.shape[1] // HEAD_DIM
    field = rows.astype(jnp.float32).reshape(count, heads, HEAD_DIM)
    field = field * lax.rsqrt(jnp.sum(field * field, axis=-1, keepdims=True) + eps_norm)
    return field.reshape(count, heads * HEAD_DIM).astype(jnp.bfloat16)


def spread_heads(weights):
    return jnp.repeat(weights, HEAD_DIM, axis=1)


def pack_round(qk, values, dest, slot, shards, cap):
    rows = qk.shape[0]
    hits = (dest[:, None] == jnp.arange(shards, dtype=jnp.int32)[None, :]).astype(jnp.int32)
    ranks = jnp.sum(hits * jnp.cumsum(hits, axis=0), axis=1) - 1
    position = dest * cap + ranks
    total = shards * cap
    send_qk = jnp.zeros((total, qk.shape[1]), qk.dtype).at[position].set(qk)
    send_values = jnp.zeros((total, values.shape[1]), values.dtype).at[position].set(values)
    send_slot = jnp.full((total,), rows, jnp.int32).at[position].set(slot)
    send_source = (
        jnp.full((total,), rows, jnp.int32).at[position].set(jnp.arange(rows, dtype=jnp.int32))
    )
    return (send_qk, send_values, send_slot, send_source)


def group_attend(queries, keys, vals):
    rows = queries.shape[0]
    heads = queries.shape[1] // HEAD_DIM
    qpart = queries.reshape(rows, heads, HEAD_DIM)
    kpart = keys.reshape(2 * rows, heads, HEAD_DIM)
    vpart = vals.reshape(2 * rows, heads, HEAD_DIM)
    scores = jnp.einsum("qhd,khd->hqk", qpart, kpart, preferred_element_type=jnp.float32)
    itself = (
        jnp.arange(2 * rows, dtype=jnp.int32)[None, :]
        == jnp.arange(rows, dtype=jnp.int32)[:, None] + rows
    )
    scores = jnp.where(itself[None], jnp.float32(self_score), scores)
    highest = jnp.max(scores, axis=-1)
    lse = highest + jnp.log(jnp.sum(jnp.exp(scores - highest[..., None]), axis=-1))
    probs = jnp.exp(scores - lse[..., None]).astype(jnp.bfloat16)
    attended = jnp.einsum("hqk,khd->qhd", probs, vpart, preferred_element_type=jnp.float32)
    return (attended.reshape(rows, heads * HEAD_DIM).astype(jnp.bfloat16), jnp.transpose(lse))


def attend_sorted(sorted_qk, sorted_values):
    rows = sorted_qk.shape[0]
    width = sorted_qk.shape[1]
    keys = unit_keys(sorted_qk)
    before_keys, before_values = passed_along((keys, sorted_values), "seq", 1)
    ext_keys = jnp.concatenate([before_keys, keys], axis=0)
    ext_values = jnp.concatenate([before_values, sorted_values], axis=0)
    group_width = width // 2

    def one_stretch(position):
        pieces = []
        totals = []
        for group in range(2):
            low = group * group_width
            high = low + group_width
            piece, total = group_attend(
                sorted_qk[:, low:high], ext_keys[:, low:high], ext_values[:, low:high]
            )
            pieces.append(piece)
            totals.append(total)
        return (jnp.concatenate(pieces, axis=1), jnp.concatenate(totals, axis=1))

    attended, lse = lax.map(one_stretch, jnp.arange(rows // STRETCH, dtype=jnp.int32))
    return (attended.reshape(rows, width), lse.reshape(rows, lse.shape[-1]))


def on_device(qk, values, dest_dev, dest_slot):
    shards = lax.axis_size("seq")
    rows = qk.shape[0]
    width = qk.shape[1]
    heads = width // HEAD_DIM
    cap = 3 * (rows // (2 * shards))
    send_qk, send_values, send_slot, send_source = pack_round(
        qk, values, dest_dev[0], dest_slot[0], shards, cap
    )
    got_qk, got_values, got_slot, got_source = (
        lax.all_to_all(send_qk, "seq", split_axis=0, concat_axis=0, tiled=True),
        lax.all_to_all(send_values, "seq", split_axis=0, concat_axis=0, tiled=True),
        lax.all_to_all(send_slot, "seq", split_axis=0, concat_axis=0, tiled=True),
        lax.all_to_all(send_source, "seq", split_axis=0, concat_axis=0, tiled=True),
    )
    sorted_qk = jnp.zeros((rows, width), jnp.bfloat16).at[got_slot].set(got_qk, mode="drop")
    sorted_values = jnp.zeros((rows, width), jnp.bfloat16).at[got_slot].set(got_values, mode="drop")
    attended, lse = attend_sorted(sorted_qk, sorted_values)
    lse = lse.reshape(rows, heads)
    picked = jnp.clip(got_slot, 0, rows - 1)
    reply_out = attended[picked]
    reply_lse = lse[picked]
    back_out, back_lse, back_ids = (
        lax.all_to_all(as_sent(reply_out), "seq", split_axis=0, concat_axis=0, tiled=True).astype(
            reply_out.dtype
        ),
        lax.all_to_all(as_sent(reply_lse), "seq", split_axis=0, concat_axis=0, tiled=True).astype(
            reply_lse.dtype
        ),
        lax.all_to_all(got_source, "seq", split_axis=0, concat_axis=0, tiled=True),
    )
    round_out = jnp.zeros((rows, width), jnp.bfloat16).at[back_ids].set(back_out, mode="drop")
    round_lse = jnp.zeros((rows, heads), jnp.float32).at[back_ids].set(back_lse, mode="drop")
    local_top = round_lse
    local_top = lax.pmax(local_top, "round")
    denom = jnp.exp(round_lse - local_top)
    numer = spread_heads(denom) * round_out.astype(jnp.float32)
    numer_half, denom_half = (
        lax.psum_scatter(
            numer.astype(jnp.bfloat16), "round", scatter_dimension=1, tiled=True
        ).astype(jnp.float32),
        lax.psum_scatter(
            denom.astype(jnp.bfloat16), "round", scatter_dimension=1, tiled=True
        ).astype(jnp.float32),
    )
    merged = numer_half / spread_heads(denom_half)
    return merged.astype(jnp.bfloat16)


NO_ROW = -1e30
STRIP = 128


def local_kernel(put_ref, tokens_ref, both, wide, keys, vals):
    blocks, _, rows, _ = tokens_ref.shape
    bound = keys.shape[0]
    moves = put_ref.shape[1]
    pairs = rows // moves

    @pl.loop(0, blocks)
    def _(block):
        for k in range(2):
            wide[pl.ds(k, rows, stride=2), :] = tokens_ref[block, k].astype(jnp.float32)

        @pl.loop(0, pairs)
        def _(group):
            line = block * pairs + group
            start = pl.multiple_of(group * (2 * moves), 2 * moves)
            for row in range(moves):
                to = put_ref[line, row]
                both[pl.ds(to, 2), :] = wide[pl.ds(start + 2 * row, 2), :]

    @pl.loop(0, bound // STRETCH)
    def _(stretch):
        low = pl.multiple_of(stretch * STRETCH, STRETCH)
        field = both[pl.ds(2 * low, STRETCH, stride=2), :]
        scale = lax.rsqrt(jnp.sum(field * field, axis=-1, keepdims=True) + eps_norm)
        keys[pl.ds(low, STRETCH), :] = (field * scale).astype(jnp.bfloat16)
        vals[pl.ds(low, STRETCH), :HEAD_DIM] = both[
            pl.ds(2 * low + 1, STRETCH, stride=2), :
        ].astype(jnp.bfloat16)
        vals[pl.ds(low, STRETCH), HEAD_DIM:] = jnp.ones((STRETCH, HEAD_DIM), jnp.bfloat16)

    row_at = lax.broadcasted_iota(jnp.int32, (STRIP, STRIP), 0)
    col_at = lax.broadcasted_iota(jnp.int32, (STRIP, STRIP), 1)

    @pl.loop(0, bound // STRETCH - 1)
    def _(stretch):
        low = pl.multiple_of(stretch * STRETCH, STRETCH)
        window = keys[pl.ds(low, 2 * STRETCH), :]
        seen = vals[pl.ds(low, 2 * STRETCH), :]
        for strip in range(0, STRETCH, STRIP):
            at = 2 * (low + STRETCH + strip)
            queries = both[pl.ds(at, STRIP, stride=2), :].astype(jnp.bfloat16)
            scores = lax.dot_general(
                queries, window, (((1,), (1,)), ((), ())), preferred_element_type=jnp.float32
            )
            left, right = STRETCH + strip, STRETCH + strip + STRIP
            pieces = [
                scores[:, :left],
                jnp.where(row_at == col_at, jnp.float32(self_score), scores[:, left:right]),
            ]
            if right < 2 * STRETCH:
                pieces.append(scores[:, right:])
            scores = jnp.concatenate(pieces, axis=1)
            highest = jnp.max(scores, axis=-1, keepdims=True)
            probs = jnp.exp(scores - highest).astype(jnp.bfloat16)
            summed = jnp.dot(probs, seen, preferred_element_type=jnp.float32)
            weight = summed[:, HEAD_DIM:]
            both[pl.ds(at, STRIP, stride=2), :] = summed[:, :HEAD_DIM] / weight
            both[pl.ds(at + 1, STRIP, stride=2), :] = highest + jnp.log(weight)

    parity = lax.rem(lax.broadcasted_iota(jnp.int32, (8, HEAD_DIM), 0), 2)
    both[pl.ds(2 * bound, 8), :] = jnp.where(parity == 0, 0.0, NO_ROW).astype(jnp.float32)


def local_attend(put, tokens, section):
    rows, wide = tokens.shape[2:]
    bound = section + STRETCH
    return pl.pallas_call(
        local_kernel,
        out_shape=jax.ShapeDtypeStruct((2 * bound + 8, wide), jnp.float32),
        in_specs=[
            pl.BlockSpec(memory_space=pltpu.SMEM),
            pl.BlockSpec(memory_space=pltpu.VMEM),
        ],
        out_specs=pl.BlockSpec(memory_space=pltpu.VMEM),
        scratch_shapes=[
            pltpu.VMEM((2 * rows, wide), jnp.float32),
            pltpu.VMEM((bound, wide), jnp.bfloat16),
            pltpu.VMEM((bound, 2 * wide), jnp.bfloat16),
        ],
        compiler_params=pltpu.CompilerParams(vmem_limit_bytes=24 * 1024 * 1024),
        name="local_attend",
    )(put, tokens)


MESH = pl.DeviceIdType.MESH


def near_first(count):
    return sorted(range(1, count), key=lambda step: min(step, count - step))


def greet_all(sides, shards, side, seat):
    barrier = pltpu.get_barrier_semaphore()
    for across in range(sides):
        for step in range(shards):
            if across or step:
                pl.semaphore_signal(
                    barrier,
                    inc=1,
                    device_id=(lax.rem(side + across, sides), lax.rem(seat + step, shards)),
                    device_id_type=MESH,
                )
    pl.semaphore_wait(barrier, sides * shards - 1)


def bring_kernel(
    plan, qk_ref, values_ref, place_ref, tokens_ref, places_ref,
    own_sem, line_send, line_recv, far_send, far_recv, near_send, near_recv, put_send, put_recv,
):
    sides, shards, heads, fars, nears = plan
    group = fars * nears
    side, seat = lax.axis_index("round"), lax.axis_index("seq")
    level, lane = seat // group, lax.rem(seat, group)
    far, near = lane // nears, lax.rem(lane, nears)

    def columns(head):
        return pl.ds(pl.multiple_of((side * heads + head) * HEAD_DIM, HEAD_DIM), HEAD_DIM)

    def seat_of(level, far, near):
        return level * group + far * nears + near

    def block_of(level, far, near):
        return (far * nears + near) * heads + level

    def remote(source, target, send, recv, to):
        return pltpu.make_async_remote_copy(
            src_ref=source, dst_ref=target, send_sem=send, recv_sem=recv,
            device_id=(side, to), device_id_type=MESH,
        )

    fields = (qk_ref, values_ref)
    mine = block_of(level, far, near)
    own = [
        pltpu.make_async_copy(fields[k].at[:, columns(level)], tokens_ref.at[mine, k], own_sem.at[k])
        for k in range(2)
    ]
    for copy in own:
        copy.start()
    greet_all(sides, shards, side, seat)

    sent = []
    line = {}
    for k in range(2):
        for step in near_first(heads):
            to = lax.rem(level + step, heads)
            copy = remote(
                fields[k].at[:, columns(to)], tokens_ref.at[mine, k],
                line_send.at[step - 1, k], line_recv.at[step - 1, k], seat_of(to, far, near),
            )
            copy.start()
            sent.append(copy)
            line[step, k] = copy

    puts = []
    for across in range(sides):
        for step in range(heads):
            for turn in range(nears):
                at = (across * heads + step) * nears + turn
                to = seat_of(lax.rem(level + step, heads), side, lax.rem(near + turn, nears))
                copy = pltpu.make_async_remote_copy(
                    src_ref=place_ref, dst_ref=places_ref.at[mine],
                    send_sem=put_send.at[at], recv_sem=put_recv.at[mine],
                    device_id=(lax.rem(side + across, sides), to), device_id_type=MESH,
                )
                puts.append(copy)
                if at:
                    copy.start()
    stays = pltpu.make_async_copy(place_ref, places_ref.at[mine], put_recv.at[mine])
    pl.when(far != side)(puts[0].start)
    pl.when(far == side)(stays.start)

    def pass_near(block, k, index):
        for turn in range(1, nears):
            copy = remote(
                tokens_ref.at[block, k], tokens_ref.at[block, k],
                near_send.at[turn - 1, index, k], near_recv.at[turn - 1, index, k],
                seat_of(level, far, lax.rem(near + turn, nears)),
            )
            copy.start()
            sent.append(copy)

    def pass_far(block, k, step):
        for turn in range(1, fars):
            copy = remote(
                tokens_ref.at[block, k], tokens_ref.at[block, k],
                far_send.at[turn - 1, step, k], far_recv.at[turn - 1, step, k],
                seat_of(level, lax.rem(far + turn, fars), near),
            )
            copy.start()
            sent.append(copy)

    def from_far(k, step):
        for turn in range(1, fars):
            source = block_of(
                lax.rem(level + heads - step, heads), lax.rem(far + fars - turn, fars), near
            )
            remote(
                tokens_ref.at[source, k], tokens_ref.at[source, k],
                far_send.at[turn - 1, step, k], far_recv.at[turn - 1, step, k], seat,
            ).wait_recv()
            pass_near(source, k, turn * heads + step)

    order = [(step, k) for k in range(2) for step in near_first(heads)]
    for k in range(2):
        own[k].wait()
        pass_far(mine, k, 0)
        pass_near(mine, k, 0)
    late = [(0, 0), (0, 1)]
    for step, k in order:
        source = block_of(lax.rem(level + heads - step, heads), far, near)
        line[step, k].wait_recv()
        pass_far(source, k, step)
        pass_near(source, k, step)
        from_far(late[0][1], late[0][0])
        late = late[1:] + [(step, k)]
    for step, k in late:
        from_far(k, step)
    for turn in range(1, nears):
        for away in range(fars):
            for step in range(heads):
                for k in range(2):
                    source = block_of(
                        lax.rem(level + heads - step, heads),
                        lax.rem(far + fars - away, fars),
                        lax.rem(near + nears - turn, nears),
                    )
                    index = away * heads + step
                    remote(
                        tokens_ref.at[source, k], tokens_ref.at[source, k],
                        near_send.at[turn - 1, index, k], near_recv.at[turn - 1, index, k], seat,
                    ).wait_recv()
    for block in range(shards):
        pltpu.make_async_copy(place_ref, places_ref.at[block], put_recv.at[block]).wait()
    for copy in sent:
        copy.wait_send()
    for copy in puts[1:]:
        copy.wait_send()
    pl.when(far != side)(puts[0].wait_send)


def bring_in(qk, values, place, plan):
    sides, shards, heads, fars, nears = plan
    rows = qk.shape[0]
    dma = pltpu.SemaphoreType.DMA
    return pl.pallas_call(
        functools.partial(bring_kernel, plan),
        out_shape=(
            jax.ShapeDtypeStruct((shards, 2, rows, HEAD_DIM), jnp.bfloat16),
            jax.ShapeDtypeStruct((shards,) + place.shape, jnp.int32),
        ),
        in_specs=[pl.BlockSpec(memory_space=pltpu.HBM)] * 2 + [pl.BlockSpec(memory_space=pltpu.VMEM)],
        out_specs=(pl.BlockSpec(memory_space=pl.ANY), pl.BlockSpec(memory_space=pl.ANY)),
        scratch_shapes=[
            dma((2,)),
            dma((heads - 1, 2)),
            dma((heads - 1, 2)),
            dma((fars - 1, heads, 2)),
            dma((fars - 1, heads, 2)),
            dma((nears - 1, fars * heads, 2)),
            dma((nears - 1, fars * heads, 2)),
            dma((sides * heads * nears,)),
            dma((shards,)),
        ],
        compiler_params=pltpu.CompilerParams(
            collective_id=0, has_side_effects=True, vmem_limit_bytes=16 * 1024 * 1024
        ),
        name="bring_in",
    )(qk, values, place)


def send_kernel(
    plan, take_ref, both_ref, out_ref,
    wide, part_ref, logs_ref, near_part, near_logs, far_part, far_logs, pass_part, pass_logs, done,
    near_send, near_recv, near_log_send, near_log_recv,
    far_send, far_recv, far_log_send, far_log_recv, line_send, line_recv,
):
    sides, shards, heads, fars, nears = plan
    group = fars * nears
    side, seat = lax.axis_index("round"), lax.axis_index("seq")
    level, lane = seat // group, lax.rem(seat, group)
    far, near = lane // nears, lax.rem(lane, nears)
    rows = part_ref.shape[1]
    moves = take_ref.shape[1]
    pairs = rows // moves

    def unsort(block):
        @pl.loop(0, pairs)
        def _(group):
            line = block * pairs + group
            start = pl.multiple_of(group * (2 * moves), 2 * moves)
            for row in range(moves):
                at = take_ref[line, row]
                wide[pl.ds(start + 2 * row, 2), :] = both_ref[pl.ds(at, 2), :]

        part_ref[block] = wide[pl.ds(0, rows, stride=2), :].astype(jnp.bfloat16)
        logs_ref[block] = jnp.transpose(wide[pl.ds(1, rows, stride=2), :])[0:1, :]

    def seat_of(level, far, near):
        return level * group + far * nears + near

    def block_of(level, far, near):
        return (far * nears + near) * heads + level

    def remote(source, target, send, recv, to):
        return pltpu.make_async_remote_copy(
            src_ref=source, dst_ref=target, send_sem=send, recv_sem=recv,
            device_id=(side, to), device_id_type=MESH,
        )

    greet_all(sides, shards, side, seat)
    steps = near_first(heads)[::-1] + [0]
    sent = []
    from_near, log_from_near = {}, {}

    def send_near(away):
        for turn in range(1, nears):
            to_near = lax.rem(near + turn, nears)
            to = seat_of(level, far, to_near)
            first = block_of(0, lax.rem(far + away, fars), to_near)
            for step in steps:
                at = away * heads + step
                block = first + lax.rem(level + step, heads)
                unsort(block)
                copy = remote(
                    part_ref.at[block], near_part.at[turn - 1, at],
                    near_send.at[turn - 1, at], near_recv.at[turn - 1, at], to,
                )
                copy.start()
                sent.append(copy)
                from_near[turn, at] = copy
            copy = remote(
                logs_ref.at[pl.ds(first, heads)], near_logs.at[turn - 1, away],
                near_log_send.at[turn - 1, away], near_log_recv.at[turn - 1, away], to,
            )
            copy.start()
            sent.append(copy)
            log_from_near[turn, away] = copy

    def logs_here(away):
        first = block_of(0, lax.rem(far + away, fars), near)
        total = logs_ref[pl.ds(first, heads)]
        for turn in range(1, nears):
            log_from_near[turn, away].wait_recv()
            total = jnp.maximum(total, near_logs[turn - 1, away])
        return total

    def part_here(away, step):
        at = away * heads + step
        block = block_of(lax.rem(level + step, heads), lax.rem(far + away, fars), near)
        unsort(block)
        total = part_ref[block].astype(jnp.float32)
        for turn in range(1, nears):
            from_near[turn, at].wait_recv()
            total = total + near_part[turn - 1, at].astype(jnp.float32)
        return total

    from_far, log_from_far = {}, {}
    for away in range(1, fars):
        send_near(away)
        to = seat_of(level, lax.rem(far + away, fars), near)
        for step in steps:
            pass_part[away - 1, step] = part_here(away, step).astype(jnp.bfloat16)
            copy = remote(
                pass_part.at[away - 1, step], far_part.at[away - 1, step],
                far_send.at[away - 1, step], far_recv.at[away - 1, step], to,
            )
            copy.start()
            sent.append(copy)
            from_far[away, step] = copy
        pass_logs[away] = logs_here(away)
        copy = remote(
            pass_logs.at[away], far_logs.at[away - 1],
            far_log_send.at[away - 1], far_log_recv.at[away - 1], to,
        )
        copy.start()
        sent.append(copy)
        log_from_far[away] = copy
    send_near(0)
    for step in steps:
        pass_part[fars - 1, step] = part_here(0, step).astype(jnp.bfloat16)
    pass_logs[0] = logs_here(0)

    for away in range(1, fars):
        log_from_far[away].wait_recv()

    def spread(weight):
        return jnp.transpose(jnp.broadcast_to(weight, (HEAD_DIM, rows)))

    from_line = []
    for step in steps:
        to = lax.rem(level + step, heads)
        logs = [pass_logs[0, to]] + [far_logs[away - 1, to] for away in range(1, fars)]
        highest = functools.reduce(jnp.maximum, logs)
        weights = [jnp.exp(log - highest) for log in logs]
        total = functools.reduce(jnp.add, weights)
        merged = spread(weights[0] / total) * pass_part[fars - 1, step].astype(jnp.float32)
        for away in range(1, fars):
            share = spread(weights[away] / total)
            from_far[away, step].wait_recv()
            merged = merged + share * far_part[away - 1, step].astype(jnp.float32)
        columns = pl.ds(pl.multiple_of(level * HEAD_DIM, HEAD_DIM), HEAD_DIM)
        if step:
            done[step - 1] = merged.astype(jnp.bfloat16)
            copy = remote(
                done.at[step - 1], out_ref.at[:, columns],
                line_send.at[step - 1], line_recv.at[step - 1], seat_of(to, far, near),
            )
            copy.start()
            sent.append(copy)
            from_line.append(copy)
        else:
            out_ref[:, columns] = merged.astype(jnp.bfloat16)
    for copy in from_line:
        copy.wait_recv()
    for copy in sent:
        copy.wait_send()


def send_back(take, both, rows, plan):
    sides, shards, heads, fars, nears = plan
    dma = pltpu.SemaphoreType.DMA

    def held(*lead):
        return pltpu.VMEM(lead + (rows, HEAD_DIM), jnp.bfloat16)

    def logs_held(*lead):
        return pltpu.VMEM(lead + (heads, 1, rows), jnp.float32)

    near_shape, far_shape = (nears - 1, fars * heads), (fars - 1, heads)
    return pl.pallas_call(
        functools.partial(send_kernel, plan),
        out_shape=jax.ShapeDtypeStruct((rows, heads * HEAD_DIM), jnp.bfloat16),
        in_specs=[
            pl.BlockSpec(memory_space=pltpu.SMEM),
            pl.BlockSpec(memory_space=pltpu.VMEM),
        ],
        out_specs=pl.BlockSpec(memory_space=pltpu.VMEM),
        scratch_shapes=[
            pltpu.VMEM((2 * rows, HEAD_DIM), jnp.float32),
            held(shards), pltpu.VMEM((shards, 1, rows), jnp.float32),
            held(*near_shape), logs_held(nears - 1, fars),
            held(*far_shape), logs_held(fars - 1),
            held(fars, heads), logs_held(fars),
            held(heads - 1),
            dma(near_shape), dma(near_shape), dma((nears - 1, fars)), dma((nears - 1, fars)),
            dma(far_shape), dma(far_shape), dma((fars - 1,)), dma((fars - 1,)),
            dma((heads - 1,)), dma((heads - 1,)),
        ],
        compiler_params=pltpu.CompilerParams(
            collective_id=1, has_side_effects=True, vmem_limit_bytes=24 * 1024 * 1024
        ),
        name="send_back",
    )(take, both)


def slots_of(place, section, base, total):
    bound = section + STRETCH
    put = jnp.minimum(lax.rem(place - base + STRETCH + total, total), bound)
    take = jnp.where(put < STRETCH, bound, put)
    return 2 * put, 2 * take


def by_heads_on_device(qk, values, dest_dev, dest_slot):
    shards = lax.axis_size("seq")
    sides = lax.axis_size("round")
    rows, width = qk.shape
    heads = width // HEAD_DIM // sides
    total = rows * shards
    group = shards // heads
    parts = group // sides
    section = total // parts
    lane = lax.rem(lax.axis_index("seq"), group)
    place = dest_dev[0] * rows + dest_slot[0]
    plan = (sides, shards, heads, sides, parts)
    tokens, places = bring_in(qk, values, place.reshape(-1, HEAD_DIM), plan)
    put, take = slots_of(places.reshape(-1, HEAD_DIM), section, lax.rem(lane, parts) * section, total)
    both = local_attend(put, tokens, section)
    return send_back(take, both, rows, plan)


def whole_head_fits(qk, shards, sides):
    rows, width = qk.shape
    heads = width // HEAD_DIM // sides
    bytes_held = rows * HEAD_DIM * shards * 2 * 2
    if shards % heads or (shards // heads) % sides:
        return False
    parts = shards // heads // sides
    if (rows * shards) % (parts * STRETCH) or parts < 2:
        return False
    return bytes_held <= 8 * 1024 * 1024


def either_plan(qk, values, dest_dev, dest_slot):
    if whole_head_fits(qk, lax.axis_size("seq"), lax.axis_size("round")):
        return by_heads_on_device(qk, values, dest_dev, dest_slot)
    return on_device(qk, values, dest_dev, dest_slot)


def solution(mesh):
    return jax.shard_map(
        either_plan,
        mesh=mesh,
        in_specs=(P("seq", None), P("seq", None), P("round", "seq"), P("round", "seq")),
        out_specs=P("seq", "round"),
        check_vma=False,
    )
```

```python
import functools

import jax
import jax.numpy as jnp
from jax import lax
from jax.experimental import pallas as pl
from jax.experimental.pallas import tpu as pltpu
from jax.sharding import PartitionSpec as P

HEAD_DIM = 128
STRETCH = 512


eps_norm = 1e-06
self_score = -100000.0


def passed_along(value, axis, steps):
    count = lax.axis_size(axis)
    pairs = [(source, (source + steps) % count) for source in range(count)]
    return lax.ppermute(value, axis, pairs)


def as_sent(array):
    return jax.tree.map(lambda a: a.astype(jnp.bfloat16) if a.dtype == jnp.float32 else a, array)


def unit_keys(rows):
    count = rows.shape[0]
    heads = rows.shape[1] // HEAD_DIM
    field = rows.astype(jnp.float32).reshape(count, heads, HEAD_DIM)
    field = field * lax.rsqrt(jnp.sum(field * field, axis=-1, keepdims=True) + eps_norm)
    return field.reshape(count, heads * HEAD_DIM).astype(jnp.bfloat16)


def spread_heads(weights):
    return jnp.repeat(weights, HEAD_DIM, axis=1)


def pack_round(qk, values, dest, slot, shards, cap):
    rows = qk.shape[0]
    hits = (dest[:, None] == jnp.arange(shards, dtype=jnp.int32)[None, :]).astype(jnp.int32)
    ranks = jnp.sum(hits * jnp.cumsum(hits, axis=0), axis=1) - 1
    position = dest * cap + ranks
    total = shards * cap
    send_qk = jnp.zeros((total, qk.shape[1]), qk.dtype).at[position].set(qk)
    send_values = jnp.zeros((total, values.shape[1]), values.dtype).at[position].set(values)
    send_slot = jnp.full((total,), rows, jnp.int32).at[position].set(slot)
    send_source = (
        jnp.full((total,), rows, jnp.int32).at[position].set(jnp.arange(rows, dtype=jnp.int32))
    )
    return (send_qk, send_values, send_slot, send_source)


def group_attend(queries, keys, vals):
    rows = queries.shape[0]
    heads = queries.shape[1] // HEAD_DIM
    qpart = queries.reshape(rows, heads, HEAD_DIM)
    kpart = keys.reshape(2 * rows, heads, HEAD_DIM)
    vpart = vals.reshape(2 * rows, heads, HEAD_DIM)
    scores = jnp.einsum("qhd,khd->hqk", qpart, kpart, preferred_element_type=jnp.float32)
    itself = (
        jnp.arange(2 * rows, dtype=jnp.int32)[None, :]
        == jnp.arange(rows, dtype=jnp.int32)[:, None] + rows
    )
    scores = jnp.where(itself[None], jnp.float32(self_score), scores)
    highest = jnp.max(scores, axis=-1)
    lse = highest + jnp.log(jnp.sum(jnp.exp(scores - highest[..., None]), axis=-1))
    probs = jnp.exp(scores - lse[..., None]).astype(jnp.bfloat16)
    attended = jnp.einsum("hqk,khd->qhd", probs, vpart, preferred_element_type=jnp.float32)
    return (attended.reshape(rows, heads * HEAD_DIM).astype(jnp.bfloat16), jnp.transpose(lse))


def attend_sorted(sorted_qk, sorted_values):
    rows = sorted_qk.shape[0]
    width = sorted_qk.shape[1]
    keys = unit_keys(sorted_qk)
    before_keys, before_values = passed_along((keys, sorted_values), "seq", 1)
    ext_keys = jnp.concatenate([before_keys, keys], axis=0)
    ext_values = jnp.concatenate([before_values, sorted_values], axis=0)
    group_width = width // 2

    def one_stretch(position):
        pieces = []
        totals = []
        for group in range(2):
            low = group * group_width
            high = low + group_width
            piece, total = group_attend(
                sorted_qk[:, low:high], ext_keys[:, low:high], ext_values[:, low:high]
            )
            pieces.append(piece)
            totals.append(total)
        return (jnp.concatenate(pieces, axis=1), jnp.concatenate(totals, axis=1))

    attended, lse = lax.map(one_stretch, jnp.arange(rows // STRETCH, dtype=jnp.int32))
    return (attended.reshape(rows, width), lse.reshape(rows, lse.shape[-1]))


def on_device(qk, values, dest_dev, dest_slot):
    shards = lax.axis_size("seq")
    rows = qk.shape[0]
    width = qk.shape[1]
    heads = width // HEAD_DIM
    cap = 3 * (rows // (2 * shards))
    send_qk, send_values, send_slot, send_source = pack_round(
        qk, values, dest_dev[0], dest_slot[0], shards, cap
    )
    got_qk, got_values, got_slot, got_source = (
        lax.all_to_all(send_qk, "seq", split_axis=0, concat_axis=0, tiled=True),
        lax.all_to_all(send_values, "seq", split_axis=0, concat_axis=0, tiled=True),
        lax.all_to_all(send_slot, "seq", split_axis=0, concat_axis=0, tiled=True),
        lax.all_to_all(send_source, "seq", split_axis=0, concat_axis=0, tiled=True),
    )
    sorted_qk = jnp.zeros((rows, width), jnp.bfloat16).at[got_slot].set(got_qk, mode="drop")
    sorted_values = jnp.zeros((rows, width), jnp.bfloat16).at[got_slot].set(got_values, mode="drop")
    attended, lse = attend_sorted(sorted_qk, sorted_values)
    lse = lse.reshape(rows, heads)
    picked = jnp.clip(got_slot, 0, rows - 1)
    reply_out = attended[picked]
    reply_lse = lse[picked]
    back_out, back_lse, back_ids = (
        lax.all_to_all(as_sent(reply_out), "seq", split_axis=0, concat_axis=0, tiled=True).astype(
            reply_out.dtype
        ),
        lax.all_to_all(as_sent(reply_lse), "seq", split_axis=0, concat_axis=0, tiled=True).astype(
            reply_lse.dtype
        ),
        lax.all_to_all(got_source, "seq", split_axis=0, concat_axis=0, tiled=True),
    )
    round_out = jnp.zeros((rows, width), jnp.bfloat16).at[back_ids].set(back_out, mode="drop")
    round_lse = jnp.zeros((rows, heads), jnp.float32).at[back_ids].set(back_lse, mode="drop")
    local_top = round_lse
    local_top = lax.pmax(local_top, "round")
    denom = jnp.exp(round_lse - local_top)
    numer = spread_heads(denom) * round_out.astype(jnp.float32)
    numer_half, denom_half = (
        lax.psum_scatter(
            numer.astype(jnp.bfloat16), "round", scatter_dimension=1, tiled=True
        ).astype(jnp.float32),
        lax.psum_scatter(
            denom.astype(jnp.bfloat16), "round", scatter_dimension=1, tiled=True
        ).astype(jnp.float32),
    )
    merged = numer_half / spread_heads(denom_half)
    return merged.astype(jnp.bfloat16)


NO_ROW = -1e30
STRIP = 128


def local_kernel(put_ref, tokens_ref, both, wide, keys, vals):
    blocks, _, rows, _ = tokens_ref.shape
    bound = keys.shape[0]
    moves = put_ref.shape[1]
    pairs = rows // moves

    @pl.loop(0, blocks)
    def _(block):
        for k in range(2):
            wide[pl.ds(k, rows, stride=2), :] = tokens_ref[block, k].astype(jnp.float32)

        @pl.loop(0, pairs)
        def _(group):
            line = block * pairs + group
            start = pl.multiple_of(group * (2 * moves), 2 * moves)
            for row in range(moves):
                to = put_ref[line, row]
                both[pl.ds(to, 2), :] = wide[pl.ds(start + 2 * row, 2), :]

    @pl.loop(0, bound // STRETCH)
    def _(stretch):
        low = pl.multiple_of(stretch * STRETCH, STRETCH)
        field = both[pl.ds(2 * low, STRETCH, stride=2), :]
        scale = lax.rsqrt(jnp.sum(field * field, axis=-1, keepdims=True) + eps_norm)
        keys[pl.ds(low, STRETCH), :] = (field * scale).astype(jnp.bfloat16)
        vals[pl.ds(low, STRETCH), :HEAD_DIM] = both[
            pl.ds(2 * low + 1, STRETCH, stride=2), :
        ].astype(jnp.bfloat16)
        vals[pl.ds(low, STRETCH), HEAD_DIM:] = jnp.ones((STRETCH, HEAD_DIM), jnp.bfloat16)

    row_at = lax.broadcasted_iota(jnp.int32, (STRIP, STRIP), 0)
    col_at = lax.broadcasted_iota(jnp.int32, (STRIP, STRIP), 1)

    @pl.loop(0, bound // STRETCH - 1)
    def _(stretch):
        low = pl.multiple_of(stretch * STRETCH, STRETCH)
        window = keys[pl.ds(low, 2 * STRETCH), :]
        seen = vals[pl.ds(low, 2 * STRETCH), :]
        for strip in range(0, STRETCH, STRIP):
            at = 2 * (low + STRETCH + strip)
            queries = both[pl.ds(at, STRIP, stride=2), :].astype(jnp.bfloat16)
            scores = lax.dot_general(
                queries, window, (((1,), (1,)), ((), ())), preferred_element_type=jnp.float32
            )
            left, right = STRETCH + strip, STRETCH + strip + STRIP
            pieces = [
                scores[:, :left],
                jnp.where(row_at == col_at, jnp.float32(self_score), scores[:, left:right]),
            ]
            if right < 2 * STRETCH:
                pieces.append(scores[:, right:])
            scores = jnp.concatenate(pieces, axis=1)
            highest = jnp.max(scores, axis=-1, keepdims=True)
            probs = jnp.exp(scores - highest).astype(jnp.bfloat16)
            summed = jnp.dot(probs, seen, preferred_element_type=jnp.float32)
            weight = summed[:, HEAD_DIM:]
            both[pl.ds(at, STRIP, stride=2), :] = summed[:, :HEAD_DIM] / weight
            both[pl.ds(at + 1, STRIP, stride=2), :] = highest + jnp.log(weight)

    parity = lax.rem(lax.broadcasted_iota(jnp.int32, (8, HEAD_DIM), 0), 2)
    both[pl.ds(2 * bound, 8), :] = jnp.where(parity == 0, 0.0, NO_ROW).astype(jnp.float32)


def local_attend(put, tokens, section):
    rows, wide = tokens.shape[2:]
    bound = section + STRETCH
    return pl.pallas_call(
        local_kernel,
        out_shape=jax.ShapeDtypeStruct((2 * bound + 8, wide), jnp.float32),
        in_specs=[
            pl.BlockSpec(memory_space=pltpu.SMEM),
            pl.BlockSpec(memory_space=pltpu.VMEM),
        ],
        out_specs=pl.BlockSpec(memory_space=pltpu.VMEM),
        scratch_shapes=[
            pltpu.VMEM((2 * rows, wide), jnp.float32),
            pltpu.VMEM((bound, wide), jnp.bfloat16),
            pltpu.VMEM((bound, 2 * wide), jnp.bfloat16),
        ],
        compiler_params=pltpu.CompilerParams(vmem_limit_bytes=24 * 1024 * 1024),
        name="local_attend",
    )(put, tokens)


MESH = pl.DeviceIdType.MESH


def near_first(count):
    return sorted(range(1, count), key=lambda step: min(step, count - step))


def greet_all(sides, shards, side, seat):
    barrier = pltpu.get_barrier_semaphore()
    for across in range(sides):
        for step in range(shards):
            if across or step:
                pl.semaphore_signal(
                    barrier,
                    inc=1,
                    device_id=(lax.rem(side + across, sides), lax.rem(seat + step, shards)),
                    device_id_type=MESH,
                )
    pl.semaphore_wait(barrier, sides * shards - 1)


def bring_kernel(
    plan, qk_ref, values_ref, place_ref, tokens_ref, places_ref,
    own_sem, line_send, line_recv, far_send, far_recv, near_send, near_recv, put_send, put_recv,
):
    sides, shards, heads, fars, nears = plan
    group = fars * nears
    side, seat = lax.axis_index("round"), lax.axis_index("seq")
    level, lane = seat // group, lax.rem(seat, group)
    far, near = lane // nears, lax.rem(lane, nears)

    def columns(head):
        return pl.ds(pl.multiple_of((side * heads + head) * HEAD_DIM, HEAD_DIM), HEAD_DIM)

    def seat_of(level, far, near):
        return level * group + far * nears + near

    def block_of(level, far, near):
        return (far * nears + near) * heads + level

    def remote(source, target, send, recv, to):
        return pltpu.make_async_remote_copy(
            src_ref=source, dst_ref=target, send_sem=send, recv_sem=recv,
            device_id=(side, to), device_id_type=MESH,
        )

    fields = (qk_ref, values_ref)
    mine = block_of(level, far, near)
    own = [
        pltpu.make_async_copy(fields[k].at[:, columns(level)], tokens_ref.at[mine, k], own_sem.at[k])
        for k in range(2)
    ]
    for copy in own:
        copy.start()
    greet_all(sides, shards, side, seat)

    sent = []
    line = {}
    for k in range(2):
        for step in near_first(heads):
            to = lax.rem(level + step, heads)
            copy = remote(
                fields[k].at[:, columns(to)], tokens_ref.at[mine, k],
                line_send.at[step - 1, k], line_recv.at[step - 1, k], seat_of(to, far, near),
            )
            copy.start()
            sent.append(copy)
            line[step, k] = copy

    puts = []
    for across in range(sides):
        for step in range(heads):
            for turn in range(nears):
                at = (across * heads + step) * nears + turn
                to = seat_of(lax.rem(level + step, heads), side, lax.rem(near + turn, nears))
                copy = pltpu.make_async_remote_copy(
                    src_ref=place_ref, dst_ref=places_ref.at[mine],
                    send_sem=put_send.at[at], recv_sem=put_recv.at[mine],
                    device_id=(lax.rem(side + across, sides), to), device_id_type=MESH,
                )
                puts.append(copy)
                if at:
                    copy.start()
    stays = pltpu.make_async_copy(place_ref, places_ref.at[mine], put_recv.at[mine])
    pl.when(far != side)(puts[0].start)
    pl.when(far == side)(stays.start)

    def pass_near(block, k, index):
        for turn in range(1, nears):
            copy = remote(
                tokens_ref.at[block, k], tokens_ref.at[block, k],
                near_send.at[turn - 1, index, k], near_recv.at[turn - 1, index, k],
                seat_of(level, far, lax.rem(near + turn, nears)),
            )
            copy.start()
            sent.append(copy)

    def pass_far(block, k, step):
        for turn in range(1, fars):
            copy = remote(
                tokens_ref.at[block, k], tokens_ref.at[block, k],
                far_send.at[turn - 1, step, k], far_recv.at[turn - 1, step, k],
                seat_of(level, lax.rem(far + turn, fars), near),
            )
            copy.start()
            sent.append(copy)

    def from_far(k, step):
        for turn in range(1, fars):
            source = block_of(
                lax.rem(level + heads - step, heads), lax.rem(far + fars - turn, fars), near
            )
            remote(
                tokens_ref.at[source, k], tokens_ref.at[source, k],
                far_send.at[turn - 1, step, k], far_recv.at[turn - 1, step, k], seat,
            ).wait_recv()
            pass_near(source, k, turn * heads + step)

    order = [(step, k) for k in range(2) for step in near_first(heads)]
    for k in range(2):
        own[k].wait()
        pass_far(mine, k, 0)
        pass_near(mine, k, 0)
    late = [(0, 0), (0, 1)]
    for step, k in order:
        source = block_of(lax.rem(level + heads - step, heads), far, near)
        line[step, k].wait_recv()
        pass_far(source, k, step)
        pass_near(source, k, step)
        from_far(late[0][1], late[0][0])
        late = late[1:] + [(step, k)]
    for step, k in late:
        from_far(k, step)
    for turn in range(1, nears):
        for away in range(fars):
            for step in range(heads):
                for k in range(2):
                    source = block_of(
                        lax.rem(level + heads - step, heads),
                        lax.rem(far + fars - away, fars),
                        lax.rem(near + nears - turn, nears),
                    )
                    index = away * heads + step
                    remote(
                        tokens_ref.at[source, k], tokens_ref.at[source, k],
                        near_send.at[turn - 1, index, k], near_recv.at[turn - 1, index, k], seat,
                    ).wait_recv()
    for block in range(shards):
        pltpu.make_async_copy(place_ref, places_ref.at[block], put_recv.at[block]).wait()
    for copy in sent:
        copy.wait_send()
    for copy in puts[1:]:
        copy.wait_send()
    pl.when(far != side)(puts[0].wait_send)


def bring_in(qk, values, place, plan):
    sides, shards, heads, fars, nears = plan
    rows = qk.shape[0]
    dma = pltpu.SemaphoreType.DMA
    return pl.pallas_call(
        functools.partial(bring_kernel, plan),
        out_shape=(
            jax.ShapeDtypeStruct((shards, 2, rows, HEAD_DIM), jnp.bfloat16),
            jax.ShapeDtypeStruct((shards,) + place.shape, jnp.int32),
        ),
        in_specs=[pl.BlockSpec(memory_space=pltpu.HBM)] * 2 + [pl.BlockSpec(memory_space=pltpu.VMEM)],
        out_specs=(pl.BlockSpec(memory_space=pl.ANY), pl.BlockSpec(memory_space=pl.ANY)),
        scratch_shapes=[
            dma((2,)),
            dma((heads - 1, 2)),
            dma((heads - 1, 2)),
            dma((fars - 1, heads, 2)),
            dma((fars - 1, heads, 2)),
            dma((nears - 1, fars * heads, 2)),
            dma((nears - 1, fars * heads, 2)),
            dma((sides * heads * nears,)),
            dma((shards,)),
        ],
        compiler_params=pltpu.CompilerParams(
            collective_id=0, has_side_effects=True, vmem_limit_bytes=16 * 1024 * 1024
        ),
        name="bring_in",
    )(qk, values, place)


def send_kernel(
    plan, take_ref, both_ref, out_ref,
    wide, part_ref, logs_ref, near_part, near_logs, far_part, far_logs, pass_part, pass_logs, done,
    near_send, near_recv, near_log_send, near_log_recv,
    far_send, far_recv, far_log_send, far_log_recv, line_send, line_recv,
):
    sides, shards, heads, fars, nears = plan
    group = fars * nears
    side, seat = lax.axis_index("round"), lax.axis_index("seq")
    level, lane = seat // group, lax.rem(seat, group)
    far, near = lane // nears, lax.rem(lane, nears)
    rows = part_ref.shape[1]
    moves = take_ref.shape[1]
    pairs = rows // moves

    def unsort(block):
        @pl.loop(0, pairs)
        def _(group):
            line = block * pairs + group
            start = pl.multiple_of(group * (2 * moves), 2 * moves)
            for row in range(moves):
                at = take_ref[line, row]
                wide[pl.ds(start + 2 * row, 2), :] = both_ref[pl.ds(at, 2), :]

        part_ref[block] = wide[pl.ds(0, rows, stride=2), :].astype(jnp.bfloat16)
        logs_ref[block] = jnp.transpose(wide[pl.ds(1, rows, stride=2), :])[0:1, :]

    def seat_of(level, far, near):
        return level * group + far * nears + near

    def block_of(level, far, near):
        return (far * nears + near) * heads + level

    def remote(source, target, send, recv, to):
        return pltpu.make_async_remote_copy(
            src_ref=source, dst_ref=target, send_sem=send, recv_sem=recv,
            device_id=(side, to), device_id_type=MESH,
        )

    greet_all(sides, shards, side, seat)
    steps = near_first(heads)[::-1] + [0]
    sent = []
    from_near, from_far = {}, {}

    def start(*copies):
        for copy in copies:
            copy.start()
            sent.append(copy)
        return copies

    def send_near(away, step):
        at = away * heads + step
        for turn in range(1, nears):
            to_near = lax.rem(near + turn, nears)
            to = seat_of(level, far, to_near)
            block = block_of(lax.rem(level + step, heads), lax.rem(far + away, fars), to_near)
            unsort(block)
            from_near[turn, at] = start(
                remote(
                    part_ref.at[block], near_part.at[turn - 1, at],
                    near_send.at[turn - 1, at], near_recv.at[turn - 1, at], to,
                ),
                remote(
                    logs_ref.at[block], near_logs.at[turn - 1, at],
                    near_log_send.at[turn - 1, at], near_log_recv.at[turn - 1, at], to,
                ),
            )

    def here(away, step):
        at = away * heads + step
        block = block_of(lax.rem(level + step, heads), lax.rem(far + away, fars), near)
        unsort(block)
        part = part_ref[block].astype(jnp.float32)
        log = logs_ref[block]
        for turn in range(1, nears):
            for copy in from_near[turn, at]:
                copy.wait_recv()
            part = part + near_part[turn - 1, at].astype(jnp.float32)
            log = jnp.maximum(log, near_logs[turn - 1, at])
        return part, log

    for away in range(1, fars):
        to = seat_of(level, lax.rem(far + away, fars), near)
        for step in steps:
            send_near(away, step)
        for step in steps:
            part, log = here(away, step)
            pass_part[away - 1, step] = part.astype(jnp.bfloat16)
            pass_logs[away - 1, step] = log
            from_far[away, step] = start(
                remote(
                    pass_part.at[away - 1, step], far_part.at[away - 1, step],
                    far_send.at[away - 1, step], far_recv.at[away - 1, step], to,
                ),
                remote(
                    pass_logs.at[away - 1, step], far_logs.at[away - 1, step],
                    far_log_send.at[away - 1, step], far_log_recv.at[away - 1, step], to,
                ),
            )
    for step in steps:
        send_near(0, step)

    def spread(weight):
        return jnp.transpose(jnp.broadcast_to(weight, (HEAD_DIM, rows)))

    from_line = []
    for step in steps:
        to = lax.rem(level + step, heads)
        part, log = here(0, step)
        parts, logs = [part], [log]
        for away in range(1, fars):
            for copy in from_far[away, step]:
                copy.wait_recv()
            parts.append(far_part[away - 1, step].astype(jnp.float32))
            logs.append(far_logs[away - 1, step])
        highest = functools.reduce(jnp.maximum, logs)
        weights = [jnp.exp(log - highest) for log in logs]
        total = functools.reduce(jnp.add, weights)
        merged = functools.reduce(
            jnp.add, [spread(weight / total) * part for weight, part in zip(weights, parts)]
        )
        columns = pl.ds(pl.multiple_of(level * HEAD_DIM, HEAD_DIM), HEAD_DIM)
        if step:
            done[step - 1] = merged.astype(jnp.bfloat16)
            copy = remote(
                done.at[step - 1], out_ref.at[:, columns],
                line_send.at[step - 1], line_recv.at[step - 1], seat_of(to, far, near),
            )
            copy.start()
            sent.append(copy)
            from_line.append(copy)
        else:
            out_ref[:, columns] = merged.astype(jnp.bfloat16)
    for copy in from_line:
        copy.wait_recv()
    for copy in sent:
        copy.wait_send()


def send_back(take, both, rows, plan):
    sides, shards, heads, fars, nears = plan
    dma = pltpu.SemaphoreType.DMA

    def held(*lead):
        return pltpu.VMEM(lead + (rows, HEAD_DIM), jnp.bfloat16)

    def logs_held(*lead):
        return pltpu.VMEM(lead + (1, rows), jnp.float32)

    near_shape, far_shape = (nears - 1, fars * heads), (fars - 1, heads)
    return pl.pallas_call(
        functools.partial(send_kernel, plan),
        out_shape=jax.ShapeDtypeStruct((rows, heads * HEAD_DIM), jnp.bfloat16),
        in_specs=[
            pl.BlockSpec(memory_space=pltpu.SMEM),
            pl.BlockSpec(memory_space=pltpu.VMEM),
        ],
        out_specs=pl.BlockSpec(memory_space=pltpu.VMEM),
        scratch_shapes=[
            pltpu.VMEM((2 * rows, HEAD_DIM), jnp.float32),
            held(shards), logs_held(shards),
            held(*near_shape), logs_held(*near_shape),
            held(*far_shape), logs_held(*far_shape),
            held(*far_shape), logs_held(*far_shape),
            held(heads - 1),
            dma(near_shape), dma(near_shape), dma(near_shape), dma(near_shape),
            dma(far_shape), dma(far_shape), dma(far_shape), dma(far_shape),
            dma((heads - 1,)), dma((heads - 1,)),
        ],
        compiler_params=pltpu.CompilerParams(
            collective_id=1, has_side_effects=True, vmem_limit_bytes=24 * 1024 * 1024
        ),
        name="send_back",
    )(take, both)


def slots_of(place, section, base, total):
    bound = section + STRETCH
    put = jnp.minimum(lax.rem(place - base + STRETCH + total, total), bound)
    take = jnp.where(put < STRETCH, bound, put)
    return 2 * put, 2 * take


def by_heads_on_device(qk, values, dest_dev, dest_slot):
    shards = lax.axis_size("seq")
    sides = lax.axis_size("round")
    rows, width = qk.shape
    heads = width // HEAD_DIM // sides
    total = rows * shards
    group = shards // heads
    parts = group // sides
    section = total // parts
    lane = lax.rem(lax.axis_index("seq"), group)
    place = dest_dev[0] * rows + dest_slot[0]
    plan = (sides, shards, heads, sides, parts)
    tokens, places = bring_in(qk, values, place.reshape(-1, HEAD_DIM), plan)
    put, take = slots_of(places.reshape(-1, HEAD_DIM), section, lax.rem(lane, parts) * section, total)
    both = local_attend(put, tokens, section)
    return send_back(take, both, rows, plan)


def whole_head_fits(qk, shards, sides):
    rows, width = qk.shape
    heads = width // HEAD_DIM // sides
    bytes_held = rows * HEAD_DIM * shards * 2 * 2
    if shards % heads or (shards // heads) % sides:
        return False
    parts = shards // heads // sides
    if (rows * shards) % (parts * STRETCH) or parts < 2:
        return False
    return bytes_held <= 8 * 1024 * 1024


def either_plan(qk, values, dest_dev, dest_slot):
    if whole_head_fits(qk, lax.axis_size("seq"), lax.axis_size("round")):
        return by_heads_on_device(qk, values, dest_dev, dest_slot)
    return on_device(qk, values, dest_dev, dest_slot)


def solution(mesh):
    return jax.shard_map(
        either_plan,
        mesh=mesh,
        in_specs=(P("seq", None), P("seq", None), P("round", "seq"), P("round", "seq")),
        out_specs=P("seq", "round"),
        check_vma=False,
    )
```

```python
import functools

import jax
import jax.numpy as jnp
from jax import lax
from jax.experimental import pallas as pl
from jax.experimental.pallas import tpu as pltpu
from jax.sharding import PartitionSpec as P

HEAD_DIM = 128
STRETCH = 512


eps_norm = 1e-06
self_score = -100000.0


def passed_along(value, axis, steps):
    count = lax.axis_size(axis)
    pairs = [(source, (source + steps) % count) for source in range(count)]
    return lax.ppermute(value, axis, pairs)


def as_sent(array):
    return jax.tree.map(lambda a: a.astype(jnp.bfloat16) if a.dtype == jnp.float32 else a, array)


def unit_keys(rows):
    count = rows.shape[0]
    heads = rows.shape[1] // HEAD_DIM
    field = rows.astype(jnp.float32).reshape(count, heads, HEAD_DIM)
    field = field * lax.rsqrt(jnp.sum(field * field, axis=-1, keepdims=True) + eps_norm)
    return field.reshape(count, heads * HEAD_DIM).astype(jnp.bfloat16)


def spread_heads(weights):
    return jnp.repeat(weights, HEAD_DIM, axis=1)


def pack_round(qk, values, dest, slot, shards, cap):
    rows = qk.shape[0]
    hits = (dest[:, None] == jnp.arange(shards, dtype=jnp.int32)[None, :]).astype(jnp.int32)
    ranks = jnp.sum(hits * jnp.cumsum(hits, axis=0), axis=1) - 1
    position = dest * cap + ranks
    total = shards * cap
    send_qk = jnp.zeros((total, qk.shape[1]), qk.dtype).at[position].set(qk)
    send_values = jnp.zeros((total, values.shape[1]), values.dtype).at[position].set(values)
    send_slot = jnp.full((total,), rows, jnp.int32).at[position].set(slot)
    send_source = (
        jnp.full((total,), rows, jnp.int32).at[position].set(jnp.arange(rows, dtype=jnp.int32))
    )
    return (send_qk, send_values, send_slot, send_source)


def group_attend(queries, keys, vals):
    rows = queries.shape[0]
    heads = queries.shape[1] // HEAD_DIM
    qpart = queries.reshape(rows, heads, HEAD_DIM)
    kpart = keys.reshape(2 * rows, heads, HEAD_DIM)
    vpart = vals.reshape(2 * rows, heads, HEAD_DIM)
    scores = jnp.einsum("qhd,khd->hqk", qpart, kpart, preferred_element_type=jnp.float32)
    itself = (
        jnp.arange(2 * rows, dtype=jnp.int32)[None, :]
        == jnp.arange(rows, dtype=jnp.int32)[:, None] + rows
    )
    scores = jnp.where(itself[None], jnp.float32(self_score), scores)
    highest = jnp.max(scores, axis=-1)
    lse = highest + jnp.log(jnp.sum(jnp.exp(scores - highest[..., None]), axis=-1))
    probs = jnp.exp(scores - lse[..., None]).astype(jnp.bfloat16)
    attended = jnp.einsum("hqk,khd->qhd", probs, vpart, preferred_element_type=jnp.float32)
    return (attended.reshape(rows, heads * HEAD_DIM).astype(jnp.bfloat16), jnp.transpose(lse))


def attend_sorted(sorted_qk, sorted_values):
    rows = sorted_qk.shape[0]
    width = sorted_qk.shape[1]
    keys = unit_keys(sorted_qk)
    before_keys, before_values = passed_along((keys, sorted_values), "seq", 1)
    ext_keys = jnp.concatenate([before_keys, keys], axis=0)
    ext_values = jnp.concatenate([before_values, sorted_values], axis=0)
    group_width = width // 2

    def one_stretch(position):
        pieces = []
        totals = []
        for group in range(2):
            low = group * group_width
            high = low + group_width
            piece, total = group_attend(
                sorted_qk[:, low:high], ext_keys[:, low:high], ext_values[:, low:high]
            )
            pieces.append(piece)
            totals.append(total)
        return (jnp.concatenate(pieces, axis=1), jnp.concatenate(totals, axis=1))

    attended, lse = lax.map(one_stretch, jnp.arange(rows // STRETCH, dtype=jnp.int32))
    return (attended.reshape(rows, width), lse.reshape(rows, lse.shape[-1]))


def on_device(qk, values, dest_dev, dest_slot):
    shards = lax.axis_size("seq")
    rows = qk.shape[0]
    width = qk.shape[1]
    heads = width // HEAD_DIM
    cap = 3 * (rows // (2 * shards))
    send_qk, send_values, send_slot, send_source = pack_round(
        qk, values, dest_dev[0], dest_slot[0], shards, cap
    )
    got_qk, got_values, got_slot, got_source = (
        lax.all_to_all(send_qk, "seq", split_axis=0, concat_axis=0, tiled=True),
        lax.all_to_all(send_values, "seq", split_axis=0, concat_axis=0, tiled=True),
        lax.all_to_all(send_slot, "seq", split_axis=0, concat_axis=0, tiled=True),
        lax.all_to_all(send_source, "seq", split_axis=0, concat_axis=0, tiled=True),
    )
    sorted_qk = jnp.zeros((rows, width), jnp.bfloat16).at[got_slot].set(got_qk, mode="drop")
    sorted_values = jnp.zeros((rows, width), jnp.bfloat16).at[got_slot].set(got_values, mode="drop")
    attended, lse = attend_sorted(sorted_qk, sorted_values)
    lse = lse.reshape(rows, heads)
    picked = jnp.clip(got_slot, 0, rows - 1)
    reply_out = attended[picked]
    reply_lse = lse[picked]
    back_out, back_lse, back_ids = (
        lax.all_to_all(as_sent(reply_out), "seq", split_axis=0, concat_axis=0, tiled=True).astype(
            reply_out.dtype
        ),
        lax.all_to_all(as_sent(reply_lse), "seq", split_axis=0, concat_axis=0, tiled=True).astype(
            reply_lse.dtype
        ),
        lax.all_to_all(got_source, "seq", split_axis=0, concat_axis=0, tiled=True),
    )
    round_out = jnp.zeros((rows, width), jnp.bfloat16).at[back_ids].set(back_out, mode="drop")
    round_lse = jnp.zeros((rows, heads), jnp.float32).at[back_ids].set(back_lse, mode="drop")
    local_top = round_lse
    local_top = lax.pmax(local_top, "round")
    denom = jnp.exp(round_lse - local_top)
    numer = spread_heads(denom) * round_out.astype(jnp.float32)
    numer_half, denom_half = (
        lax.psum_scatter(
            numer.astype(jnp.bfloat16), "round", scatter_dimension=1, tiled=True
        ).astype(jnp.float32),
        lax.psum_scatter(
            denom.astype(jnp.bfloat16), "round", scatter_dimension=1, tiled=True
        ).astype(jnp.float32),
    )
    merged = numer_half / spread_heads(denom_half)
    return merged.astype(jnp.bfloat16)


NO_ROW = -1e30
STRIP = 128


def local_kernel(put_ref, tokens_ref, both, wide, keys, vals):
    blocks, _, rows, _ = tokens_ref.shape
    bound = keys.shape[0]
    moves = put_ref.shape[1]
    pairs = rows // moves

    @pl.loop(0, blocks)
    def _(block):
        for k in range(2):
            wide[pl.ds(k, rows, stride=2), :] = tokens_ref[block, k].astype(jnp.float32)

        @pl.loop(0, pairs)
        def _(group):
            line = block * pairs + group
            start = pl.multiple_of(group * (2 * moves), 2 * moves)
            for row in range(moves):
                to = put_ref[line, row]
                both[pl.ds(to, 2), :] = wide[pl.ds(start + 2 * row, 2), :]

    @pl.loop(0, bound // STRETCH)
    def _(stretch):
        low = pl.multiple_of(stretch * STRETCH, STRETCH)
        field = both[pl.ds(2 * low, STRETCH, stride=2), :]
        scale = lax.rsqrt(jnp.sum(field * field, axis=-1, keepdims=True) + eps_norm)
        keys[pl.ds(low, STRETCH), :] = (field * scale).astype(jnp.bfloat16)
        vals[pl.ds(low, STRETCH), :HEAD_DIM] = both[
            pl.ds(2 * low + 1, STRETCH, stride=2), :
        ].astype(jnp.bfloat16)
        vals[pl.ds(low, STRETCH), HEAD_DIM:] = jnp.ones((STRETCH, HEAD_DIM), jnp.bfloat16)

    row_at = lax.broadcasted_iota(jnp.int32, (STRIP, STRIP), 0)
    col_at = lax.broadcasted_iota(jnp.int32, (STRIP, STRIP), 1)

    @pl.loop(0, bound // STRETCH - 1)
    def _(stretch):
        low = pl.multiple_of(stretch * STRETCH, STRETCH)
        window = keys[pl.ds(low, 2 * STRETCH), :]
        seen = vals[pl.ds(low, 2 * STRETCH), :]
        for strip in range(0, STRETCH, STRIP):
            at = 2 * (low + STRETCH + strip)
            queries = both[pl.ds(at, STRIP, stride=2), :].astype(jnp.bfloat16)
            scores = lax.dot_general(
                queries, window, (((1,), (1,)), ((), ())), preferred_element_type=jnp.float32
            )
            left, right = STRETCH + strip, STRETCH + strip + STRIP
            pieces = [
                scores[:, :left],
                jnp.where(row_at == col_at, jnp.float32(self_score), scores[:, left:right]),
            ]
            if right < 2 * STRETCH:
                pieces.append(scores[:, right:])
            scores = jnp.concatenate(pieces, axis=1)
            highest = jnp.max(scores, axis=-1, keepdims=True)
            probs = jnp.exp(scores - highest).astype(jnp.bfloat16)
            summed = jnp.dot(probs, seen, preferred_element_type=jnp.float32)
            weight = summed[:, HEAD_DIM:]
            both[pl.ds(at, STRIP, stride=2), :] = summed[:, :HEAD_DIM] / weight
            both[pl.ds(at + 1, STRIP, stride=2), :] = highest + jnp.log(weight)

    parity = lax.rem(lax.broadcasted_iota(jnp.int32, (8, HEAD_DIM), 0), 2)
    both[pl.ds(2 * bound, 8), :] = jnp.where(parity == 0, 0.0, NO_ROW).astype(jnp.float32)


def local_attend(put, tokens, section):
    rows, wide = tokens.shape[2:]
    bound = section + STRETCH
    return pl.pallas_call(
        local_kernel,
        out_shape=jax.ShapeDtypeStruct((2 * bound + 8, wide), jnp.float32),
        in_specs=[
            pl.BlockSpec(memory_space=pltpu.SMEM),
            pl.BlockSpec(memory_space=pltpu.VMEM),
        ],
        out_specs=pl.BlockSpec(memory_space=pltpu.VMEM),
        scratch_shapes=[
            pltpu.VMEM((2 * rows, wide), jnp.float32),
            pltpu.VMEM((bound, wide), jnp.bfloat16),
            pltpu.VMEM((bound, 2 * wide), jnp.bfloat16),
        ],
        compiler_params=pltpu.CompilerParams(vmem_limit_bytes=24 * 1024 * 1024),
        name="local_attend",
    )(put, tokens)


MESH = pl.DeviceIdType.MESH


def near_first(count):
    return sorted(range(1, count), key=lambda step: min(step, count - step))


def greet_all(sides, shards, side, seat):
    barrier = pltpu.get_barrier_semaphore()
    for across in range(sides):
        for step in range(shards):
            if across or step:
                pl.semaphore_signal(
                    barrier,
                    inc=1,
                    device_id=(lax.rem(side + across, sides), lax.rem(seat + step, shards)),
                    device_id_type=MESH,
                )
    pl.semaphore_wait(barrier, sides * shards - 1)


def bring_kernel(
    plan, qk_ref, values_ref, place_ref, tokens_ref, places_ref,
    own_sem, line_send, line_recv, far_send, far_recv, near_send, near_recv, put_send, put_recv,
):
    sides, shards, heads, fars, nears = plan
    group = fars * nears
    side, seat = lax.axis_index("round"), lax.axis_index("seq")
    level, lane = seat // group, lax.rem(seat, group)
    far, near = lane // nears, lax.rem(lane, nears)

    def columns(head):
        return pl.ds(pl.multiple_of((side * heads + head) * HEAD_DIM, HEAD_DIM), HEAD_DIM)

    def seat_of(level, far, near):
        return level * group + far * nears + near

    def block_of(level, far, near):
        return (far * nears + near) * heads + level

    def remote(source, target, send, recv, to):
        return pltpu.make_async_remote_copy(
            src_ref=source, dst_ref=target, send_sem=send, recv_sem=recv,
            device_id=(side, to), device_id_type=MESH,
        )

    fields = (qk_ref, values_ref)
    mine = block_of(level, far, near)
    own = [
        pltpu.make_async_copy(fields[k].at[:, columns(level)], tokens_ref.at[mine, k], own_sem.at[k])
        for k in range(2)
    ]
    for copy in own:
        copy.start()
    greet_all(sides, shards, side, seat)

    sent = []
    line = {}
    for k in range(2):
        for step in near_first(heads)[::-1]:
            to = lax.rem(level + step, heads)
            copy = remote(
                fields[k].at[:, columns(to)], tokens_ref.at[mine, k],
                line_send.at[step - 1, k], line_recv.at[step - 1, k], seat_of(to, far, near),
            )
            copy.start()
            sent.append(copy)
            line[step, k] = copy

    puts = []
    for across in range(sides):
        for step in range(heads):
            for turn in range(nears):
                at = (across * heads + step) * nears + turn
                to = seat_of(lax.rem(level + step, heads), side, lax.rem(near + turn, nears))
                copy = pltpu.make_async_remote_copy(
                    src_ref=place_ref, dst_ref=places_ref.at[mine],
                    send_sem=put_send.at[at], recv_sem=put_recv.at[mine],
                    device_id=(lax.rem(side + across, sides), to), device_id_type=MESH,
                )
                puts.append(copy)
                if at:
                    copy.start()
    stays = pltpu.make_async_copy(place_ref, places_ref.at[mine], put_recv.at[mine])
    pl.when(far != side)(puts[0].start)
    pl.when(far == side)(stays.start)

    def pass_near(block, k, index):
        for turn in range(1, nears):
            copy = remote(
                tokens_ref.at[block, k], tokens_ref.at[block, k],
                near_send.at[turn - 1, index, k], near_recv.at[turn - 1, index, k],
                seat_of(level, far, lax.rem(near + turn, nears)),
            )
            copy.start()
            sent.append(copy)

    def pass_far(block, k, step):
        for turn in range(1, fars):
            copy = remote(
                tokens_ref.at[block, k], tokens_ref.at[block, k],
                far_send.at[turn - 1, step, k], far_recv.at[turn - 1, step, k],
                seat_of(level, lax.rem(far + turn, fars), near),
            )
            copy.start()
            sent.append(copy)

    def from_far(k, step):
        for turn in range(1, fars):
            source = block_of(
                lax.rem(level + heads - step, heads), lax.rem(far + fars - turn, fars), near
            )
            remote(
                tokens_ref.at[source, k], tokens_ref.at[source, k],
                far_send.at[turn - 1, step, k], far_recv.at[turn - 1, step, k], seat,
            ).wait_recv()
            pass_near(source, k, turn * heads + step)

    order = [(step, k) for k in range(2) for step in near_first(heads)[::-1]]
    for k in range(2):
        own[k].wait()
        pass_far(mine, k, 0)
        pass_near(mine, k, 0)
    late = [(0, 0), (0, 1)]
    for step, k in order:
        source = block_of(lax.rem(level + heads - step, heads), far, near)
        line[step, k].wait_recv()
        pass_far(source, k, step)
        pass_near(source, k, step)
        from_far(late[0][1], late[0][0])
        late = late[1:] + [(step, k)]
    for step, k in late:
        from_far(k, step)
    for turn in range(1, nears):
        for away in range(fars):
            for step in range(heads):
                for k in range(2):
                    source = block_of(
                        lax.rem(level + heads - step, heads),
                        lax.rem(far + fars - away, fars),
                        lax.rem(near + nears - turn, nears),
                    )
                    index = away * heads + step
                    remote(
                        tokens_ref.at[source, k], tokens_ref.at[source, k],
                        near_send.at[turn - 1, index, k], near_recv.at[turn - 1, index, k], seat,
                    ).wait_recv()
    for block in range(shards):
        pltpu.make_async_copy(place_ref, places_ref.at[block], put_recv.at[block]).wait()
    for copy in sent:
        copy.wait_send()
    for copy in puts[1:]:
        copy.wait_send()
    pl.when(far != side)(puts[0].wait_send)


def bring_in(qk, values, place, plan):
    sides, shards, heads, fars, nears = plan
    rows = qk.shape[0]
    dma = pltpu.SemaphoreType.DMA
    return pl.pallas_call(
        functools.partial(bring_kernel, plan),
        out_shape=(
            jax.ShapeDtypeStruct((shards, 2, rows, HEAD_DIM), jnp.bfloat16),
            jax.ShapeDtypeStruct((shards,) + place.shape, jnp.int32),
        ),
        in_specs=[pl.BlockSpec(memory_space=pltpu.HBM)] * 2 + [pl.BlockSpec(memory_space=pltpu.VMEM)],
        out_specs=(pl.BlockSpec(memory_space=pl.ANY), pl.BlockSpec(memory_space=pl.ANY)),
        scratch_shapes=[
            dma((2,)),
            dma((heads - 1, 2)),
            dma((heads - 1, 2)),
            dma((fars - 1, heads, 2)),
            dma((fars - 1, heads, 2)),
            dma((nears - 1, fars * heads, 2)),
            dma((nears - 1, fars * heads, 2)),
            dma((sides * heads * nears,)),
            dma((shards,)),
        ],
        compiler_params=pltpu.CompilerParams(
            collective_id=0, has_side_effects=True, vmem_limit_bytes=16 * 1024 * 1024
        ),
        name="bring_in",
    )(qk, values, place)


def send_kernel(
    plan, take_ref, both_ref, out_ref,
    wide, part_ref, logs_ref, near_part, near_logs, far_part, far_logs, pass_part, pass_logs, done,
    near_send, near_recv, near_log_send, near_log_recv,
    far_send, far_recv, far_log_send, far_log_recv, line_send, line_recv,
):
    sides, shards, heads, fars, nears = plan
    group = fars * nears
    side, seat = lax.axis_index("round"), lax.axis_index("seq")
    level, lane = seat // group, lax.rem(seat, group)
    far, near = lane // nears, lax.rem(lane, nears)
    rows = part_ref.shape[1]
    moves = take_ref.shape[1]
    pairs = rows // moves

    def unsort(block):
        @pl.loop(0, pairs)
        def _(group):
            line = block * pairs + group
            start = pl.multiple_of(group * (2 * moves), 2 * moves)
            for row in range(moves):
                at = take_ref[line, row]
                wide[pl.ds(start + 2 * row, 2), :] = both_ref[pl.ds(at, 2), :]

        part_ref[block] = wide[pl.ds(0, rows, stride=2), :].astype(jnp.bfloat16)
        logs_ref[block] = jnp.transpose(wide[pl.ds(1, rows, stride=2), :])[0:1, :]

    def seat_of(level, far, near):
        return level * group + far * nears + near

    def block_of(level, far, near):
        return (far * nears + near) * heads + level

    def remote(source, target, send, recv, to):
        return pltpu.make_async_remote_copy(
            src_ref=source, dst_ref=target, send_sem=send, recv_sem=recv,
            device_id=(side, to), device_id_type=MESH,
        )

    greet_all(sides, shards, side, seat)
    steps = near_first(heads)[::-1] + [0]
    sent = []
    from_near, from_far = {}, {}

    def start(*copies):
        for copy in copies:
            copy.start()
            sent.append(copy)
        return copies

    def send_near(away, step):
        at = away * heads + step
        for turn in range(1, nears):
            to_near = lax.rem(near + turn, nears)
            to = seat_of(level, far, to_near)
            block = block_of(lax.rem(level + step, heads), lax.rem(far + away, fars), to_near)
            unsort(block)
            from_near[turn, at] = start(
                remote(
                    part_ref.at[block], near_part.at[turn - 1, at],
                    near_send.at[turn - 1, at], near_recv.at[turn - 1, at], to,
                ),
                remote(
                    logs_ref.at[block], near_logs.at[turn - 1, at],
                    near_log_send.at[turn - 1, at], near_log_recv.at[turn - 1, at], to,
                ),
            )

    def here(away, step):
        at = away * heads + step
        block = block_of(lax.rem(level + step, heads), lax.rem(far + away, fars), near)
        unsort(block)
        part = part_ref[block].astype(jnp.float32)
        log = logs_ref[block]
        for turn in range(1, nears):
            for copy in from_near[turn, at]:
                copy.wait_recv()
            part = part + near_part[turn - 1, at].astype(jnp.float32)
            log = jnp.maximum(log, near_logs[turn - 1, at])
        return part, log

    for away in range(1, fars):
        to = seat_of(level, lax.rem(far + away, fars), near)
        for step in steps:
            send_near(away, step)
        for step in steps:
            part, log = here(away, step)
            pass_part[away - 1, step] = part.astype(jnp.bfloat16)
            pass_logs[away - 1, step] = log
            from_far[away, step] = start(
                remote(
                    pass_part.at[away - 1, step], far_part.at[away - 1, step],
                    far_send.at[away - 1, step], far_recv.at[away - 1, step], to,
                ),
                remote(
                    pass_logs.at[away - 1, step], far_logs.at[away - 1, step],
                    far_log_send.at[away - 1, step], far_log_recv.at[away - 1, step], to,
                ),
            )
    for step in steps:
        send_near(0, step)

    def spread(weight):
        return jnp.transpose(jnp.broadcast_to(weight, (HEAD_DIM, rows)))

    from_line = []
    for step in steps:
        to = lax.rem(level + step, heads)
        part, log = here(0, step)
        parts, logs = [part], [log]
        for away in range(1, fars):
            for copy in from_far[away, step]:
                copy.wait_recv()
            parts.append(far_part[away - 1, step].astype(jnp.float32))
            logs.append(far_logs[away - 1, step])
        highest = functools.reduce(jnp.maximum, logs)
        weights = [jnp.exp(log - highest) for log in logs]
        total = functools.reduce(jnp.add, weights)
        merged = functools.reduce(
            jnp.add, [spread(weight / total) * part for weight, part in zip(weights, parts)]
        )
        columns = pl.ds(pl.multiple_of(level * HEAD_DIM, HEAD_DIM), HEAD_DIM)
        if step:
            done[step - 1] = merged.astype(jnp.bfloat16)
            copy = remote(
                done.at[step - 1], out_ref.at[:, columns],
                line_send.at[step - 1], line_recv.at[step - 1], seat_of(to, far, near),
            )
            copy.start()
            sent.append(copy)
            from_line.append(copy)
        else:
            out_ref[:, columns] = merged.astype(jnp.bfloat16)
    for copy in from_line:
        copy.wait_recv()
    for copy in sent:
        copy.wait_send()


def send_back(take, both, rows, plan):
    sides, shards, heads, fars, nears = plan
    dma = pltpu.SemaphoreType.DMA

    def held(*lead):
        return pltpu.VMEM(lead + (rows, HEAD_DIM), jnp.bfloat16)

    def logs_held(*lead):
        return pltpu.VMEM(lead + (1, rows), jnp.float32)

    near_shape, far_shape = (nears - 1, fars * heads), (fars - 1, heads)
    return pl.pallas_call(
        functools.partial(send_kernel, plan),
        out_shape=jax.ShapeDtypeStruct((rows, heads * HEAD_DIM), jnp.bfloat16),
        in_specs=[
            pl.BlockSpec(memory_space=pltpu.SMEM),
            pl.BlockSpec(memory_space=pltpu.VMEM),
        ],
        out_specs=pl.BlockSpec(memory_space=pltpu.VMEM),
        scratch_shapes=[
            pltpu.VMEM((2 * rows, HEAD_DIM), jnp.float32),
            held(shards), logs_held(shards),
            held(*near_shape), logs_held(*near_shape),
            held(*far_shape), logs_held(*far_shape),
            held(*far_shape), logs_held(*far_shape),
            held(heads - 1),
            dma(near_shape), dma(near_shape), dma(near_shape), dma(near_shape),
            dma(far_shape), dma(far_shape), dma(far_shape), dma(far_shape),
            dma((heads - 1,)), dma((heads - 1,)),
        ],
        compiler_params=pltpu.CompilerParams(
            collective_id=1, has_side_effects=True, vmem_limit_bytes=24 * 1024 * 1024
        ),
        name="send_back",
    )(take, both)


def slots_of(place, section, base, total):
    bound = section + STRETCH
    put = jnp.minimum(lax.rem(place - base + STRETCH + total, total), bound)
    take = jnp.where(put < STRETCH, bound, put)
    return 2 * put, 2 * take


def by_heads_on_device(qk, values, dest_dev, dest_slot):
    shards = lax.axis_size("seq")
    sides = lax.axis_size("round")
    rows, width = qk.shape
    heads = width // HEAD_DIM // sides
    total = rows * shards
    group = shards // heads
    parts = group // sides
    section = total // parts
    lane = lax.rem(lax.axis_index("seq"), group)
    place = dest_dev[0] * rows + dest_slot[0]
    plan = (sides, shards, heads, sides, parts)
    tokens, places = bring_in(qk, values, place.reshape(-1, HEAD_DIM), plan)
    put, take = slots_of(places.reshape(-1, HEAD_DIM), section, lax.rem(lane, parts) * section, total)
    both = local_attend(put, tokens, section)
    return send_back(take, both, rows, plan)


def whole_head_fits(qk, shards, sides):
    rows, width = qk.shape
    heads = width // HEAD_DIM // sides
    bytes_held = rows * HEAD_DIM * shards * 2 * 2
    if shards % heads or (shards // heads) % sides:
        return False
    parts = shards // heads // sides
    if (rows * shards) % (parts * STRETCH) or parts < 2:
        return False
    return bytes_held <= 8 * 1024 * 1024


def either_plan(qk, values, dest_dev, dest_slot):
    if whole_head_fits(qk, lax.axis_size("seq"), lax.axis_size("round")):
        return by_heads_on_device(qk, values, dest_dev, dest_slot)
    return on_device(qk, values, dest_dev, dest_slot)


def solution(mesh):
    return jax.shard_map(
        either_plan,
        mesh=mesh,
        in_specs=(P("seq", None), P("seq", None), P("round", "seq"), P("round", "seq")),
        out_specs=P("seq", "round"),
        check_vma=False,
    )
```
